1024 devices in a mesh: tm: 16 (over y, z_hi), rows: 8 (over z_lo), dp: 8 (over x, core).
Axes of the slice: x: 4, y: 8, z: 16 (z_hi: 2, z_lo: 8; z = z_hi * 8 + z_lo), core: 2. Of those that a mesh axis runs over, the one named last changes fastest.
Arguments:
- latent_grad: bfloat16 [589824, 64], P(('dp', 'tm'), 'rows'), parts along dimension 0, may hold values from -6 to 6
- features: bfloat16 [256, 96, 96, 384], P(('dp', 'tm'), 'rows'), parts along dimension 0, may hold values from -6 to 6
- head_weight: bfloat16 [432, 384], replicated, may hold values from -0.0625 to 0.0625
Outputs:
- grad_features: bfloat16 [256, 96, 96, 384], P(('dp', 'tm'), 'rows'), parts along dimension 0
- head_weight_grad: float32 [3456, 384], P('dp'), parts along dimension 0
The draws below stay inside these ranges and needn't reach their ends.
There are 8 independent parts, one for each index of `dp`. The reference program is written for one: setup_inputs(seed, part) draws one part's arguments, and reference() takes and returns one part's arrays. A program takes and returns all parts, laid end to end along the dimension named above; an argument that names none is the same for every part. Nothing has to cross between parts.
All inputs are finite; a program needn't handle non-finite values.
Results may differ from the reference program's by a relative error of at most 0.0031.
Values may be sent and summed in bfloat16 or wider, within the bound.
A program may use at most 64 MiB of HBM per device.

```python
import math
import jax
import jax.numpy as jnp
from jax import lax

C = 384
CL = 16
W = 96
NT = 32
NH = 96
FEAT = 64
TOKENS = 73728
TOK_TM = 4608
N_TM = 16


def block_scale(own_key, extent, cuts, low, high):
    factor_of, own = 1.0, jax.random.fold_in(own_key, 6)
    for axis_at, shards_of in cuts:
        draws = jnp.exp(jax.random.uniform(jax.random.fold_in(own, axis_at), (shards_of,), jnp.float32, low / len(cuts), high / len(cuts)))
        factor_of = factor_of * jnp.repeat(draws, extent[axis_at] // shards_of).reshape([-1 if axis == axis_at else 1 for axis in range(len(extent))])
    return factor_of


def noise(key, shape, spread, reach, shards=(), kind=jnp.bfloat16):
    loudness = block_scale(key, shape, shards, -0.22, 0.18) if shards else 1.0
    values = jax.random.normal(key, shape, jnp.float32) * spread * loudness
    return jnp.minimum(jnp.maximum(values, -reach), reach).astype(kind)


def setup_inputs(seed: int = 0, part: int = 0) -> dict:
    seeds = jax.random.split(jax.random.key(seed), 4)
    part_keys = jax.random.split(jax.random.fold_in(seeds[3], part), 4)
    return {
        "latent_grad": noise(part_keys[0], (TOKENS, FEAT), 1.0, 6.0, ((0, 16), (1, 8))),
        "features": noise(part_keys[1], (NT, NH, W, C), 1.0, 6.0, ((0, 16), (1, 8))),
        "head_weight": noise(seeds[2], (27 * CL, C), (27 * C) ** -0.5, 0.0625),
    }


def to_grid(latent_grad):
    split = latent_grad.reshape(N_TM, TOK_TM // 2, 2, FEAT)
    first = split[:, :, 0]
    second = split[::-1, :, 1]
    ordered = jnp.concatenate([first, second], axis=0)
    ordered = ordered.transpose(1, 0, 2).reshape(TOKENS, FEAT)
    grid = ordered.reshape(NT, NH // 2, W // 2, CL, 2, 2)
    return grid.transpose(0, 1, 4, 2, 5, 3).reshape(NT, NH, W, CL)

def reference(latent_grad, features, head_weight):
    grid = to_grid(latent_grad)
    padded = jnp.pad(grid, ((0, 2), (1, 1), (1, 1), (0, 0)))

    def frame_step(total, frame):
        window = lax.dynamic_slice_in_dim(padded, frame, 3, 0)
        pieces = []
        for kt in range(3):
            for kh in range(3):
                for kw in range(3):
                    pieces.append(window[2 - kt, 2 - kh:2 - kh + NH, 2 - kw:2 - kw + W, :])
        cols = jnp.concatenate(pieces, axis=-1).reshape(NH * W, 27 * CL)
        hidden = lax.dynamic_index_in_dim(features, frame, 0, keepdims=False).reshape(NH * W, C).astype(jnp.float32)
        sig = jax.nn.sigmoid(hidden)
        act = (hidden * sig).astype(jnp.bfloat16)
        pre = jnp.dot(cols, head_weight, preferred_element_type=jnp.float32)
        grads = (pre * sig * (1.0 + hidden * (1.0 - sig))).astype(jnp.bfloat16)
        term = lax.dot_general(cols, act, (((0,), (0,)), ((), ())), preferred_element_type=jnp.float32)
        return (total + term, grads.reshape(NH, W, C))
    start = jnp.zeros((27 * CL, C), jnp.float32)
    total, grad_features = lax.scan(frame_step, start, jnp.arange(NT, dtype=jnp.int32))
    scale = 1.0 / math.sqrt(NT * NH * W)
    return (grad_features, total * scale)
```

```python
import math

import jax
import jax.numpy as jnp
from jax import lax
from jax.experimental import pallas as pl
from jax.experimental.pallas import tpu as pltpu
from jax.sharding import PartitionSpec as P

NY = 8
NZ = 16
OWN = 11
MESH = pl.DeviceIdType.MESH
Y_ORDER = (4, 3, 5, 2, 6, 1, 7)
Z_ORDER = (8, 7, 9, 6, 10, 5, 11, 4, 12, 3, 13, 2, 14, 1, 15)


def kernel(scale, lat, feat, weight, grad_out, sum_out, xf, act, dsl, gout, lp, send, rx1, rx2, perm, ts, os_, gt, cols, sb, rb, sb2, rb2, az, ay, in_sem, out_sem, loc_sem, sa, ra, sz, rz, sc, rc, sd, rd, se, re, sf, rf):
    tm = lax.axis_index("tm")
    rows = lax.axis_index("rows")
    y = lax.div(tm, 2)
    zh = lax.rem(tm, 2)
    z = zh * 8 + rows

    def y_dev(d):
        other = lax.rem(y + d, NY)
        return other, {"tm": other * 2 + zh}

    def z_dev(d):
        other = lax.rem(z + d, NZ)
        return other, {"tm": y * 2 + lax.div(other, 8), "rows": lax.rem(other, 8)}

    load = pltpu.make_async_copy(feat, xf, in_sem)
    load.start()

    barrier = pltpu.get_barrier_semaphore()
    for d in range(1, NY):
        pl.semaphore_signal(barrier, inc=1, device_id=y_dev(d)[1], device_id_type=MESH)
    for d in range(1, NZ):
        pl.semaphore_signal(barrier, inc=1, device_id=z_dev(d)[1], device_id_type=MESH)

    lp[:, 0:128] = jnp.zeros((8, 128), jnp.float32)
    lp[:, 128:4736] = lat[...].astype(jnp.float32)
    lp[:, 4736:5248] = jnp.zeros((8, 512), jnp.float32)
    lane8 = lax.broadcasted_iota(jnp.int32, (8, 128), 1)

    def pack(pair, carry):
        base = pl.multiple_of(pair * 1152, 128)
        for y2 in range(2):
            for zd in range(16):
                value = jnp.zeros((8, 128), jnp.float32)
                for tt in range(4):
                    start = 128 + 576 * y2 + 288 * (zd // 8) + 144 * tt + 18 * (zd % 8) - 6
                    v, l = start // 128, start % 128
                    shift = (32 * tt - l) % 128
                    piece = lp[:, pl.ds(base + 128 * v, 128)]
                    piece = pltpu.roll(piece, shift, 1) if shift else piece
                    if l > 96:
                        nxt = lp[:, pl.ds(base + 128 * v + 128, 128)]
                        nxt = pltpu.roll(nxt, shift, 1) if shift else nxt
                        piece = jnp.where(lane8 < 32 * tt + 128 - l, piece, nxt)
                    value = piece if tt == 0 else jnp.where(lane8 < 32 * tt, value, piece)
                send[pair * 2 + y2, zd] = value.astype(jnp.bfloat16)
        return carry

    lax.fori_loop(0, 4, pack, 0)
    pl.semaphore_wait(barrier, NY + NZ - 2)

    first = []
    for d in Y_ORDER:
        other, dev = y_dev(d)
        copy = pltpu.make_async_remote_copy(send.at[other], rx1.at[y], sa.at[d], ra.at[d], device_id=dev, device_id_type=MESH)
        copy.start()
        first.append(copy)
    own1 = pltpu.make_async_copy(send.at[y], rx1.at[y], loc_sem.at[0])
    own1.start()

    row = lax.broadcasted_iota(jnp.int32, (256, 256), 0)
    col = lax.broadcasted_iota(jnp.int32, (256, 256), 1)
    source = ((row >> 3) & 7) * 2 + ((row >> 6) & 1)
    token = jnp.where(row < 128, source, 31 - source)
    target = ((row >> 2) & 1) * 128 + ((row >> 1) & 1) * 64 + token * 2 + (row & 1)
    perm[...] = jnp.where(col == target, 1.0, 0.0).astype(jnp.bfloat16)

    load.wait()

    def silu(step, carry):
        at = pl.ds(pl.multiple_of(step * 64, 64), 64)
        x = xf[at, :].astype(jnp.float32)
        sig = 1.0 / (1.0 + jnp.exp(-x))
        act[at, :] = (x * sig).astype(jnp.bfloat16)
        dsl[at, :] = sig * (1.0 + x * (1.0 - sig))
        return carry

    lax.fori_loop(0, 36, silu, 0)

    own1.wait()
    for copy in first:
        copy.wait()

    second = []
    for d in Z_ORDER:
        other, dev = z_dev(d)
        copy = pltpu.make_async_remote_copy(rx1.at[:, other], rx2.at[z], sz.at[d], rz.at[d], device_id=dev, device_id_type=MESH)
        copy.start()
        second.append(copy)
    own2 = pltpu.make_async_copy(rx1.at[:, z], rx2.at[z], loc_sem.at[1])
    own2.start()
    own2.wait()
    for copy in second:
        copy.wait()

    for r in range(8):
        low = rx2[r].astype(jnp.float32).reshape(64, 128)
        high = rx2[8 + r].astype(jnp.float32).reshape(64, 128)
        ts[r] = jnp.concatenate([low, high], axis=0).T
    for r in range(8):
        even = ts[r, pl.ds(0, 64, stride=2), :]
        odd = ts[r, pl.ds(1, 64, stride=2), :]
        left = jnp.concatenate([even, odd], axis=1).astype(jnp.bfloat16)
        moved = jnp.dot(left, perm[...], preferred_element_type=jnp.float32)
        os_[0, r * 64:(r + 1) * 64, :] = moved[:, 0:128]
        os_[1, r * 64:(r + 1) * 64, :] = moved[:, 128:256]
    top = rows == 0
    bottom = rows == 7
    for t in range(4):
        for g in range(5):
            for e in range(2):
                k0, k1, k2 = [os_[e, pl.ds(t * 16 + 3 * g + k, 8, stride=64), :] for k in range(3)]
                at = pl.ds(t * 16 + e, 8, stride=2)
                k1_64 = pltpu.roll(k1, 64, 1)
                k2_96 = pltpu.roll(k2, 96, 1)
                k0_32 = pltpu.roll(k0, 32, 1)
                if g > 0:
                    v0 = jnp.where(lane8 < 64, k0, jnp.where(lane8 < 96, k1_64, k0_32))
                    if g == 4:
                        v0 = jnp.where(bottom, 0.0, v0)
                    gt[3 * g, at, :] = v0
                if 0 < g < 4:
                    v1 = jnp.where(lane8 < 64, jnp.where(lane8 < 32, k0_32, pltpu.roll(k1, 96, 1)), jnp.where(lane8 < 96, pltpu.roll(k1, 32, 1), k2_96))
                    gt[3 * g + 1, at, :] = v1
                if g < 4:
                    v2 = jnp.where(lane8 < 32, k2_96, jnp.where(lane8 < 64, k1_64, k2))
                    if g == 0:
                        v2 = jnp.where(top, 0.0, v2)
                    gt[3 * g + 2, at, :] = v2

    place = lax.rem(lax.broadcasted_iota(jnp.int32, (16, 1152), 1), 96)
    for t in range(4):
        grid = jnp.concatenate([gt[v, 16 * t:16 * t + 16, :] for v in range(2, 13)], axis=1)
        for kh in range(3):
            for kw in range(3):
                off = 128 + (1 - kh) * 96 + 1 - kw
                block = (pltpu.roll(grid, 1408 - off, 1) if off % 1408 else grid)[:, 0:1152]
                if kw == 0:
                    block = jnp.where(place == 95, 0.0, block)
                if kw == 2:
                    block = jnp.where(place == 0, 0.0, block)
                at = (3 - t) * 144 + (kh * 3 + kw) * 16
                cols[at:at + 16, :] = block.astype(jnp.bfloat16)

    for c in range(3):
        lanes = slice(128 * c, 128 * c + 128)
        total = jnp.dot(cols[144:576, :], act[0:1152, lanes], preferred_element_type=jnp.float32)
        total = total + jnp.dot(cols[0:432, :], act[1152:2304, lanes], preferred_element_type=jnp.float32)
        sb[27 * c:27 * c + 27] = total.reshape(27, 16, 128).astype(jnp.bfloat16)
    sb[81:88] = jnp.zeros((7, 16, 128), jnp.bfloat16)

    third = []
    for d in Y_ORDER:
        other, dev = y_dev(d)
        copy = pltpu.make_async_remote_copy(sb.at[pl.ds(other * OWN, OWN)], rb.at[d], sc.at[d], rc.at[d], device_id=dev, device_id_type=MESH)
        copy.start()
        third.append(copy)

    for t in range(2):
        def backward(step, carry):
            lanes = pl.ds(pl.multiple_of(step * 384, 128), 384)
            at = pl.ds(pl.multiple_of(t * 1152 + step * 384, 128), 384)
            pre = lax.dot_general(cols[(1 - t) * 144:(1 - t) * 144 + 432, lanes], weight[...], (((0,), (0,)), ((), ())), preferred_element_type=jnp.float32)
            gout[at, :] = (pre * dsl[at, :]).astype(jnp.bfloat16)
            return carry

        lax.fori_loop(0, 3, backward, 0)
    store = pltpu.make_async_copy(gout, grad_out, out_sem)
    store.start()

    for copy in third:
        copy.wait()
    part = sb[pl.ds(y * OWN, OWN)].astype(jnp.float32)
    for d in range(1, NY):
        part = part + rb[d].astype(jnp.float32)
    sb2[...] = part.astype(jnp.bfloat16)

    for d in Z_ORDER:
        other, dev = z_dev(d)

        @pl.when(other < OWN)
        def _():
            pltpu.make_async_remote_copy(sb2.at[other], rb2.at[d], sd.at[d], rd.at[d], device_id=dev, device_id_type=MESH).start()

    @pl.when(z < OWN)
    def _():
        for d in range(1, NZ):
            pltpu.make_async_remote_copy(sb2.at[0], rb2.at[d], sd.at[d], rd.at[d], device_id=z_dev(d)[1], device_id_type=MESH).wait_recv()
        whole = sb2[z].astype(jnp.float32)
        for d in range(1, NZ):
            whole = whole + rb2[d].astype(jnp.float32)
        az[z] = (whole * scale).astype(jnp.bfloat16)
        for d in Z_ORDER:
            pltpu.make_async_remote_copy(az.at[z], az.at[z], se.at[d], re.at[d], device_id=z_dev(d)[1], device_id_type=MESH).start()

    for d in range(1, NZ):
        @pl.when(lax.rem(z + NZ - d, NZ) < OWN)
        def _():
            pltpu.make_async_remote_copy(az.at[0], az.at[0], se.at[d], re.at[d], device_id=z_dev(d)[1], device_id_type=MESH).wait_recv()

    last = []
    for d in Y_ORDER:
        other, dev = y_dev(d)
        copy = pltpu.make_async_remote_copy(az, ay.at[y], sf.at[d], rf.at[d], device_id=dev, device_id_type=MESH)
        copy.start()
        last.append(copy)
    sum_out[pl.ds(y * OWN, OWN)] = az[...]
    for d in range(1, NZ):
        @pl.when(lax.rem(z + d, NZ) < OWN)
        def _():
            pltpu.make_async_remote_copy(sb2.at[0], rb2.at[d], sd.at[d], rd.at[d], device_id=z_dev(d)[1], device_id_type=MESH).wait_send()

    @pl.when(z < OWN)
    def _():
        for d in range(1, NZ):
            pltpu.make_async_remote_copy(az.at[0], az.at[0], se.at[d], re.at[d], device_id=z_dev(d)[1], device_id_type=MESH).wait_send()

    for copy in last:
        copy.wait()
    for d in range(1, NY):
        other = lax.rem(y + NY - d, NY)
        sum_out[pl.ds(other * OWN, OWN)] = ay[other]
    store.wait()


def shards(latent_grad, features, head_weight):
    frames, rows_here, width, channels = features.shape
    cells = frames * rows_here * width
    scale = 1.0 / math.sqrt(cells * NY * NZ)
    bf, f32 = jnp.bfloat16, jnp.float32
    dma = pltpu.SemaphoreType.DMA
    vmem = pl.BlockSpec(memory_space=pltpu.VMEM)
    hbm = pl.BlockSpec(memory_space=pl.ANY)
    grad, total = pl.pallas_call(
        lambda *refs: kernel(scale, *refs),
        out_shape=(
            jax.ShapeDtypeStruct((cells, channels), bf),
            jax.ShapeDtypeStruct((NY * OWN, 16, 128), bf),
        ),
        in_specs=[vmem, hbm, vmem],
        out_specs=(hbm, vmem),
        scratch_shapes=[
            pltpu.VMEM((cells, channels), bf),
            pltpu.VMEM((cells, channels), bf),
            pltpu.VMEM((cells, channels), f32),
            pltpu.VMEM((cells, channels), bf),
            pltpu.VMEM((8, 5248), f32),
            pltpu.VMEM((NY, NZ, 8, 128), bf),
            pltpu.VMEM((NY, NZ, 8, 128), bf),
            pltpu.VMEM((NZ, NY, 8, 128), bf),
            pltpu.VMEM((256, 256), bf),
            pltpu.VMEM((8, 128, 128), f32),
            pltpu.VMEM((2, 512, 128), f32),
            pltpu.VMEM((15, 64, 128), f32),
            pltpu.VMEM((576, 1152), bf),
            pltpu.VMEM((NY * OWN, 16, 128), bf),
            pltpu.VMEM((NY, OWN, 16, 128), bf),
            pltpu.VMEM((OWN, 16, 128), bf),
            pltpu.VMEM((NZ, 16, 128), bf),
            pltpu.VMEM((OWN, 16, 128), bf),
            pltpu.VMEM((NY, OWN, 16, 128), bf),
            dma, dma, dma((2,)),
            dma((NY,)), dma((NY,)), dma((NZ,)), dma((NZ,)),
            dma((NY,)), dma((NY,)), dma((NZ,)), dma((NZ,)),
            dma((NZ,)), dma((NZ,)), dma((NY,)), dma((NY,)),
        ],
        compiler_params=pltpu.CompilerParams(collective_id=0, has_side_effects=True),
        name="encoder_head_backward",
    )(latent_grad.T, features.reshape(cells, channels), head_weight)
    total = total[:81].reshape(3, 432, 128).transpose(1, 0, 2).reshape(432, 384)
    return grad.reshape(features.shape), total.astype(f32)


def solution(mesh):
    return jax.shard_map(
        shards,
        mesh=mesh,
        in_specs=(P(("dp", "tm"), "rows"), P(("dp", "tm"), "rows", None, None), P()),
        out_specs=(P(("dp", "tm"), "rows", None, None), P("dp", None)),
        check_vma=False,
    )
```

```python
import math

import jax
import jax.numpy as jnp
from jax import lax
from jax.experimental import pallas as pl
from jax.experimental.pallas import tpu as pltpu
from jax.sharding import PartitionSpec as P

NY = 8
NZ = 16
OWN_A = 14
OWN_B = 4
ALL_A = 112
USED_A = 98
MESH = pl.DeviceIdType.MESH
Y_ORDER = (4, 3, 5, 2, 6, 1, 7)
SLOTS = (0, 1, 7, 2, 6, 3, 5, 4)
GROUPS = ((0, 1), (1, 3), (3, 5), (5, 8))
Z_ORDER = (8, 7, 9, 6, 10, 5, 11, 4, 12, 3, 13, 2, 14, 1, 15)


def kernel(scale, lat_hbm, feat, weight_hbm, grad_out, sum_out, lat, weight, xf, act, dsl, gout, lp, send, rx1, rx2, perm, ts, os_, gt, cols, sa, sb, ra, rb, pa, qa, pb, qb, fin, in_sem, out_sem, sy, ry, sz, rz, s1a, r1a, s1b, r1b, s2a, r2a, s2b, r2b, s3a, r3a, s3b, r3b, s4a, r4a, s4b, r4b):
    tm = lax.axis_index("tm")
    rows = lax.axis_index("rows")
    y = lax.div(tm, 2)
    zh = lax.rem(tm, 2)
    z = zh * 8 + rows

    def y_dev(d):
        other = lax.rem(y + d, NY)
        return other, {"tm": other * 2 + zh}

    def z_dev(d):
        other = lax.rem(z + d, NZ)
        return other, {"tm": y * 2 + lax.div(other, 8), "rows": lax.rem(other, 8)}

    load_lat = pltpu.make_async_copy(lat_hbm, lat, in_sem.at[0])
    load_lat.start()
    load = pltpu.make_async_copy(feat, xf, in_sem.at[1])
    load.start()
    load_weight = pltpu.make_async_copy(weight_hbm, weight, in_sem.at[2])
    load_weight.start()

    barrier = pltpu.get_barrier_semaphore()
    for d in range(1, NY):
        pl.semaphore_signal(barrier, inc=1, device_id=y_dev(d)[1], device_id_type=MESH)
    for d in range(1, NZ):
        pl.semaphore_signal(barrier, inc=1, device_id=z_dev(d)[1], device_id_type=MESH)

    lp[:, 0:128] = jnp.zeros((8, 128), jnp.float32)
    load_lat.wait()
    lp[:, 128:4736] = lat[...].astype(jnp.float32)
    lp[:, 4736:5248] = jnp.zeros((8, 512), jnp.float32)
    lane8 = lax.broadcasted_iota(jnp.int32, (8, 128), 1)

    def pack(pair, carry):
        base = pl.multiple_of(pair * 1152, 128)
        for y2 in range(2):
            for zd in range(16):
                value = jnp.zeros((8, 128), jnp.float32)
                for tt in range(4):
                    start = 128 + 576 * y2 + 288 * (zd // 8) + 144 * tt + 18 * (zd % 8) - 6
                    v, l = start // 128, start % 128
                    shift = (32 * tt - l) % 128
                    piece = lp[:, pl.ds(base + 128 * v, 128)]
                    piece = pltpu.roll(piece, shift, 1) if shift else piece
                    if l > 96:
                        nxt = lp[:, pl.ds(base + 128 * v + 128, 128)]
                        nxt = pltpu.roll(nxt, shift, 1) if shift else nxt
                        piece = jnp.where(lane8 < 32 * tt + 128 - l, piece, nxt)
                    value = piece if tt == 0 else jnp.where(lane8 < 32 * tt, value, piece)
                send[pair * 2 + y2, zd] = value.astype(jnp.bfloat16)
        return carry

    lax.fori_loop(0, 4, pack, 0)
    pl.semaphore_wait(barrier, NY + NZ - 2)

    first = [None] * NY
    for slot in range(1, NY):
        other, dev = y_dev(SLOTS[slot])
        copy = pltpu.make_async_remote_copy(send.at[other], rx1.at[slot], sy.at[slot], ry.at[slot], device_id=dev, device_id_type=MESH)
        copy.start()
        first[slot] = copy

    second = []
    for group, (lo, hi) in enumerate(GROUPS):
        for slot in range(max(lo, 1), hi):
            first[slot].wait_recv()
        for d in Z_ORDER:
            other, dev = z_dev(d)
            source = rx1.at[lo:hi, other] if group else send.at[pl.ds(y, 1), other]
            copy = pltpu.make_async_remote_copy(source, rx2.at[z, lo:hi], sz.at[group, d], rz.at[group, d], device_id=dev, device_id_type=MESH)
            copy.start()
            second.append(copy)
    rx2[z, 0] = send[y, z]
    rx2[z, 1:8] = rx1[1:8, z]

    row = lax.broadcasted_iota(jnp.int32, (256, 256), 0)
    col = lax.broadcasted_iota(jnp.int32, (256, 256), 1)
    slot = (row >> 3) & 7
    back = jnp.where((slot & 1) == 1, (slot + 1) >> 1, 8 - (slot >> 1))
    source = ((y + 8 - back) & 7) * 2 + ((row >> 6) & 1)
    token = jnp.where(row < 128, source, 31 - source)
    target = ((row >> 2) & 1) * 128 + ((row >> 1) & 1) * 64 + token * 2 + (row & 1)
    perm[...] = jnp.where(col == target, 1.0, 0.0).astype(jnp.bfloat16)

    load.wait()

    def silu(step, carry):
        at = pl.ds(pl.multiple_of(step * 64, 64), 64)
        x = xf[at, :].astype(jnp.float32)
        sig = 1.0 / (1.0 + jnp.exp(-x))
        act[at, :] = (x * sig).astype(jnp.bfloat16)
        dsl[at, :] = sig * (1.0 + x * (1.0 - sig))
        return carry

    lax.fori_loop(0, 36, silu, 0)

    for copy in second:
        copy.wait()
    for slot in range(1, NY):
        first[slot].wait_send()

    for r in range(8):
        low = rx2[r].astype(jnp.float32).reshape(64, 128)
        high = rx2[8 + r].astype(jnp.float32).reshape(64, 128)
        ts[r] = jnp.concatenate([low, high], axis=0).T
    for r in range(8):
        even = ts[r, pl.ds(0, 64, stride=2), :]
        odd = ts[r, pl.ds(1, 64, stride=2), :]
        left = jnp.concatenate([even, odd], axis=1).astype(jnp.bfloat16)
        moved = jnp.dot(left, perm[...], preferred_element_type=jnp.float32)
        os_[0, r * 64:(r + 1) * 64, :] = moved[:, 0:128]
        os_[1, r * 64:(r + 1) * 64, :] = moved[:, 128:256]
    top = rows == 0
    bottom = rows == 7
    for t in range(4):
        for g in range(5):
            for e in range(2):
                k0, k1, k2 = [os_[e, pl.ds(t * 16 + 3 * g + k, 8, stride=64), :] for k in range(3)]
                at = pl.ds(t * 16 + e, 8, stride=2)
                k1_64 = pltpu.roll(k1, 64, 1)
                k2_96 = pltpu.roll(k2, 96, 1)
                k0_32 = pltpu.roll(k0, 32, 1)
                if g > 0:
                    v0 = jnp.where(lane8 < 64, k0, jnp.where(lane8 < 96, k1_64, k0_32))
                    if g == 4:
                        v0 = jnp.where(bottom, 0.0, v0)
                    gt[3 * g, at, :] = v0
                if 0 < g < 4:
                    v1 = jnp.where(lane8 < 64, jnp.where(lane8 < 32, k0_32, pltpu.roll(k1, 96, 1)), jnp.where(lane8 < 96, pltpu.roll(k1, 32, 1), k2_96))
                    gt[3 * g + 1, at, :] = v1
                if g < 4:
                    v2 = jnp.where(lane8 < 32, k2_96, jnp.where(lane8 < 64, k1_64, k2))
                    if g == 0:
                        v2 = jnp.where(top, 0.0, v2)
                    gt[3 * g + 2, at, :] = v2

    place = lax.rem(lax.broadcasted_iota(jnp.int32, (16, 1152), 1), 96)
    for t in range(4):
        grid = jnp.concatenate([gt[v, 16 * t:16 * t + 16, :] for v in range(2, 13)], axis=1)
        for kh in range(3):
            for kw in range(3):
                off = 128 + (1 - kh) * 96 + 1 - kw
                block = (pltpu.roll(grid, 1408 - off, 1) if off % 1408 else grid)[:, 0:1152]
                if kw == 0:
                    block = jnp.where(place == 95, 0.0, block)
                if kw == 2:
                    block = jnp.where(place == 0, 0.0, block)
                at = (3 - t) * 144 + (kh * 3 + kw) * 16
                cols[at:at + 16, :] = block.astype(jnp.bfloat16)

    for c in range(3):
        lanes = slice(128 * c, 128 * c + 128)
        total = jnp.dot(cols[144:576, :], act[0:1152, lanes], preferred_element_type=jnp.float32)
        total = total + jnp.dot(cols[0:432, :], act[1152:2304, lanes], preferred_element_type=jnp.float32)
        total = total.reshape(54, 8, 128).astype(jnp.bfloat16)
        cut = min(max(USED_A - 54 * c, 0), 54)
        if cut > 0:
            sa[54 * c:54 * c + cut] = total[0:cut]
        if cut < 54:
            at = 54 * c + cut - USED_A
            sb[at:at + 54 - cut] = total[cut:54]
    sa[USED_A:ALL_A] = jnp.zeros((ALL_A - USED_A, 8, 128), jnp.bfloat16)

    def y_copy(source, target, ssem, rsem, d):
        return pltpu.make_async_remote_copy(source, target, ssem.at[d], rsem.at[d], device_id=y_dev(d)[1], device_id_type=MESH)

    def z_copy(source, target, ssem, rsem, d):
        return pltpu.make_async_remote_copy(source, target, ssem.at[d], rsem.at[d], device_id=z_dev(d)[1], device_id_type=MESH)

    first_a = {d: y_copy(sa.at[pl.ds(y_dev(d)[0] * OWN_A, OWN_A)], ra.at[d], s1a, r1a, d) for d in Y_ORDER}
    first_b = {d: z_copy(sb.at[pl.ds(z_dev(d)[0] * OWN_B, OWN_B)], rb.at[d], s1b, r1b, d) for d in Z_ORDER}
    for copy in [*first_a.values(), *first_b.values()]:
        copy.start()

    load_weight.wait()

    def backward(t):
        def one(step, carry):
            lanes = pl.ds(pl.multiple_of(step * 384, 128), 384)
            at = pl.ds(pl.multiple_of(t * 1152 + step * 384, 128), 384)
            pre = lax.dot_general(cols[(1 - t) * 144:(1 - t) * 144 + 432, lanes], weight[...], (((0,), (0,)), ((), ())), preferred_element_type=jnp.float32)
            gout[at, :] = (pre * dsl[at, :]).astype(jnp.bfloat16)
            return carry

        lax.fori_loop(0, 3, one, 0)
        at = pl.ds(t * 1152, 1152)
        store = pltpu.make_async_copy(gout.at[at], grad_out.at[at], out_sem.at[t])
        store.start()
        return store

    stores = [backward(0)]

    for copy in first_a.values():
        copy.wait_recv()
    part = sa[pl.ds(y * OWN_A, OWN_A)].astype(jnp.float32)
    for d in range(1, NY):
        part = part + ra[d].astype(jnp.float32)
    pa[...] = part
    for d in Z_ORDER:
        @pl.when(z_dev(d)[0] < OWN_A)
        def _():
            z_copy(pa.at[z_dev(d)[0]], qa.at[d], s2a, r2a, d).start()

    for copy in first_b.values():
        copy.wait_recv()
    part = sb[pl.ds(z * OWN_B, OWN_B)].astype(jnp.float32)
    for d in range(1, NZ):
        part = part + rb[d].astype(jnp.float32)
    pb[...] = part
    for d in Y_ORDER:
        @pl.when(y_dev(d)[0] < OWN_B)
        def _():
            y_copy(pb.at[y_dev(d)[0]], qb.at[d], s2b, r2b, d).start()

    mine_a = y * OWN_A + z
    mine_b = ALL_A + z * OWN_B + y

    @pl.when(z < OWN_A)
    def _():
        for d in range(1, NZ):
            z_copy(pa.at[0], qa.at[d], s2a, r2a, d).wait_recv()
        whole = pa[z]
        for d in range(1, NZ):
            whole = whole + qa[d]
        fin[mine_a] = (whole * scale).astype(jnp.bfloat16)
        for d in Z_ORDER:
            z_copy(fin.at[mine_a], fin.at[mine_a], s3a, r3a, d).start()

    @pl.when(y < OWN_B)
    def _():
        for d in range(1, NY):
            y_copy(pb.at[0], qb.at[d], s2b, r2b, d).wait_recv()
        whole = pb[y]
        for d in range(1, NY):
            whole = whole + qb[d]
        fin[mine_b] = (whole * scale).astype(jnp.bfloat16)
        for d in Y_ORDER:
            y_copy(fin.at[mine_b], fin.at[mine_b], s3b, r3b, d).start()

    for d in range(1, NZ):
        owner = lax.rem(z + NZ - d, NZ)

        @pl.when(owner < OWN_A)
        def _():
            piece = fin.at[y * OWN_A + owner]
            z_copy(piece, piece, s3a, r3a, d).wait_recv()
    block = fin.at[pl.ds(y * OWN_A, OWN_A)]
    last_a = {d: y_copy(block, block, s4a, r4a, d) for d in Y_ORDER}
    for copy in last_a.values():
        copy.start()

    for d in range(1, NY):
        owner = lax.rem(y + NY - d, NY)

        @pl.when(owner < OWN_B)
        def _():
            piece = fin.at[ALL_A + z * OWN_B + owner]
            y_copy(piece, piece, s3b, r3b, d).wait_recv()
    block = fin.at[pl.ds(ALL_A + z * OWN_B, OWN_B)]
    last_b = {d: z_copy(block, block, s4b, r4b, d) for d in Z_ORDER}
    for copy in last_b.values():
        copy.start()

    stores.append(backward(1))

    for copy in [*first_a.values(), *first_b.values()]:
        copy.wait_send()
    for d in range(1, NZ):
        @pl.when(z_dev(d)[0] < OWN_A)
        def _():
            z_copy(pa.at[0], qa.at[d], s2a, r2a, d).wait_send()
    for d in range(1, NY):
        @pl.when(y_dev(d)[0] < OWN_B)
        def _():
            y_copy(pb.at[0], qb.at[d], s2b, r2b, d).wait_send()

    @pl.when(z < OWN_A)
    def _():
        for d in range(1, NZ):
            z_copy(fin.at[mine_a], fin.at[mine_a], s3a, r3a, d).wait_send()

    @pl.when(y < OWN_B)
    def _():
        for d in range(1, NY):
            y_copy(fin.at[mine_b], fin.at[mine_b], s3b, r3b, d).wait_send()

    for d, copy in last_a.items():
        copy.wait_send()
        landed = fin.at[pl.ds(lax.rem(y + NY - d, NY) * OWN_A, OWN_A)]
        y_copy(landed, landed, s4a, r4a, d).wait_recv()
    for d, copy in last_b.items():
        copy.wait_send()
        landed = fin.at[pl.ds(ALL_A + lax.rem(z + NZ - d, NZ) * OWN_B, OWN_B)]
        z_copy(landed, landed, s4b, r4b, d).wait_recv()
    b0 = 108 - USED_A
    sum_out[:, 0:128] = fin[0:54].astype(jnp.float32).reshape(432, 128)
    sum_out[0:432 - 8 * b0, 128:256] = fin[54:USED_A].astype(jnp.float32).reshape(432 - 8 * b0, 128)
    sum_out[432 - 8 * b0:432, 128:256] = fin[ALL_A:ALL_A + b0].astype(jnp.float32).reshape(8 * b0, 128)
    sum_out[:, 256:384] = fin[ALL_A + b0:ALL_A + b0 + 54].astype(jnp.float32).reshape(432, 128)
    for store in stores:
        store.wait()


def shards(latent_grad, features, head_weight):
    frames, rows_here, width, channels = features.shape
    cells = frames * rows_here * width
    scale = 1.0 / math.sqrt(cells * NY * NZ)
    bf, f32 = jnp.bfloat16, jnp.float32
    dma = pltpu.SemaphoreType.DMA
    vmem = pl.BlockSpec(memory_space=pltpu.VMEM)
    hbm = pl.BlockSpec(memory_space=pl.ANY)
    grad, total = pl.pallas_call(
        lambda *refs: kernel(scale, *refs),
        out_shape=(
            jax.ShapeDtypeStruct((cells, channels), bf),
            jax.ShapeDtypeStruct((432, 384), f32),
        ),
        in_specs=[hbm, hbm, hbm],
        out_specs=(hbm, vmem),
        scratch_shapes=[
            pltpu.VMEM((8, 4608), bf),
            pltpu.VMEM((432, 384), bf),
            pltpu.VMEM((cells, channels), bf),
            pltpu.VMEM((cells, channels), bf),
            pltpu.VMEM((cells, channels), f32),
            pltpu.VMEM((cells, channels), bf),
            pltpu.VMEM((8, 5248), f32),
            pltpu.VMEM((NY, NZ, 8, 128), bf),
            pltpu.VMEM((NY, NZ, 8, 128), bf),
            pltpu.VMEM((NZ, NY, 8, 128), bf),
            pltpu.VMEM((256, 256), bf),
            pltpu.VMEM((8, 128, 128), f32),
            pltpu.VMEM((2, 512, 128), f32),
            pltpu.VMEM((15, 64, 128), f32),
            pltpu.VMEM((576, 1152), bf),
            pltpu.VMEM((ALL_A, 8, 128), bf),
            pltpu.VMEM((NZ * OWN_B, 8, 128), bf),
            pltpu.VMEM((NY, OWN_A, 8, 128), bf),
            pltpu.VMEM((NZ, OWN_B, 8, 128), bf),
            pltpu.VMEM((OWN_A, 8, 128), f32),
            pltpu.VMEM((NZ, 8, 128), f32),
            pltpu.VMEM((OWN_B, 8, 128), f32),
            pltpu.VMEM((NY, 8, 128), f32),
            pltpu.VMEM((ALL_A + NZ * OWN_B, 8, 128), bf),
            dma((3,)), dma((2,)),
            dma((NY,)), dma((NY,)), dma((len(GROUPS), NZ)), dma((len(GROUPS), NZ)),
            dma((NY,)), dma((NY,)), dma((NZ,)), dma((NZ,)),
            dma((NZ,)), dma((NZ,)), dma((NY,)), dma((NY,)),
            dma((NZ,)), dma((NZ,)), dma((NY,)), dma((NY,)),
            dma((NY,)), dma((NY,)), dma((NZ,)), dma((NZ,)),
        ],
        compiler_params=pltpu.CompilerParams(collective_id=0, has_side_effects=True),
        name="encoder_head_backward",
    )(latent_grad.T, features.reshape(cells, channels), head_weight)
    return grad.reshape(features.shape), total


def solution(mesh):
    return jax.shard_map(
        shards,
        mesh=mesh,
        in_specs=(P(("dp", "tm"), "rows"), P(("dp", "tm"), "rows", None, None), P()),
        out_specs=(P(("dp", "tm"), "rows", None, None), P("dp", None)),
        check_vma=False,
    )
```

```python
import math

import jax
import jax.numpy as jnp
from jax import lax
from jax.experimental import pallas as pl
from jax.experimental.pallas import tpu as pltpu
from jax.sharding import PartitionSpec as P

NY = 8
NZ = 16
OWN_A = 14
OWN_B = 4
ALL_A = 112
USED_A = 98
MESH = pl.DeviceIdType.MESH
Y_ORDER = (4, 3, 5, 2, 6, 1, 7)
SLOTS = (0, 1, 7, 2, 6, 3, 5, 4)
Z_LOWER = (7, 6, 8, 5, 9, 4, 10, 3, 11, 2, 12, 1, 13, 0, 14)
GROUPS = ((0, 1), (1, 3), (3, 5), (5, 8))
Z_ORDER = (8, 7, 9, 6, 10, 5, 11, 4, 12, 3, 13, 2, 14, 1, 15)


def kernel(scale, lat_hbm, feat, weight_hbm, grad_out, sum_out, weight, xf, act, dsl, lp, pk, rx1, rx2, perm, ts, os_, gt, cols, sa, sb, ra, rb, pa, qa, pb, qb, fin, in_sem, ready, sy, ry, sz, rz, s1a, r1a, s1b, r1b, s2a, r2a, s2b, r2b, s3a, r3a, s3b, r3b, s4a, r4a, s4b, r4b):
    tm = lax.axis_index("tm")
    rows = lax.axis_index("rows")
    y = lax.div(tm, 2)
    zh = lax.rem(tm, 2)
    z = zh * 8 + rows

    def y_dev(d):
        other = lax.rem(y + d, NY)
        return other, {"tm": other * 2 + zh}

    def z_dev(d):
        other = lax.rem(z + d, NZ)
        return other, {"tm": y * 2 + lax.div(other, 8), "rows": lax.rem(other, 8)}

    def z_at(other):
        return {"tm": y * 2 + other // 8, "rows": other % 8}

    def window(other):
        first_tile = jnp.minimum(lax.div(9 * other, 2), 28)
        return lat_hbm.at[:, pl.ds(pl.multiple_of(first_tile * 128, 128), 1024)]

    own = pltpu.make_async_copy(window(y), rx1.at[0, :, 0:1024], in_sem.at[0])
    own.start()
    load = pltpu.make_async_copy(feat, xf, in_sem.at[1])
    load.start()
    load_weight = pltpu.make_async_copy(weight_hbm, weight, in_sem.at[2])
    load_weight.start()

    barrier = pltpu.get_barrier_semaphore()
    for d in range(1, NY):
        pl.semaphore_signal(barrier, inc=1, device_id=y_dev(d)[1], device_id_type=MESH)
    for other in range(1, NZ):
        @pl.when(other > z)
        def _():
            pl.semaphore_signal(barrier, inc=1, device_id=z_at(other), device_id_type=MESH)
    rx1[:, :, 1024:1408] = jnp.zeros((NY, 8, 384), jnp.bfloat16)
    lp[:, 0:128] = jnp.zeros((8, 128), jnp.float32)
    pl.semaphore_wait(barrier, NY - 1 + z)

    first = [None] * NY
    for slot in range(1, NY):
        other, dev = y_dev(SLOTS[slot])
        copy = pltpu.make_async_remote_copy(window(other), rx1.at[slot, :, 0:1024], sy.at[slot], ry.at[slot], device_id=dev, device_id_type=MESH)
        copy.start()
        first[slot] = copy
    for other in range(NZ - 1):
        @pl.when(other < z)
        def _():
            pl.semaphore_signal(ready.at[z], inc=1, device_id=z_at(other), device_id_type=MESH)

    lane8 = lax.broadcasted_iota(jnp.int32, (8, 128), 1)
    base = pl.multiple_of(jnp.where(y == NY - 1, 384, 0), 128)
    odd = lax.rem(y, 2) == 1

    def pack(slot, carry):
        tiles = [rx1[slot, :, pl.ds(base + 128 * j, 128)].astype(jnp.float32) for j in range(8)]
        turned = [pltpu.roll(tile, 64, 1) for tile in tiles]
        for j in range(7):
            lp[:, 128 * j + 128:128 * j + 256] = jnp.where(odd, jnp.where(lane8 < 64, turned[j], turned[j + 1]), tiles[j])
        for zd in range(NZ):
            value = None
            for tt in range(4):
                start = 128 + 288 * (zd // 8) + 144 * tt + 18 * (zd % 8) - 6
                v, l = start // 128, start % 128
                shift = (32 * tt - l) % 128
                piece = lp[:, 128 * v:128 * v + 128]
                piece = pltpu.roll(piece, shift, 1) if shift else piece
                if l > 96:
                    nxt = lp[:, 128 * v + 128:128 * v + 256]
                    nxt = pltpu.roll(nxt, shift, 1) if shift else nxt
                    piece = jnp.where(lane8 < 32 * tt + 128 - l, piece, nxt)
                value = piece if tt == 0 else jnp.where(lane8 < 32 * tt, value, piece)
            pk[slot, zd] = value.astype(jnp.bfloat16)
        return carry

    def part_copy(group, other, source):
        lo, hi = GROUPS[group]
        return pltpu.make_async_remote_copy(pk.at[lo:hi, other], rx2.at[source, lo:hi], sz.at[group, other], rz.at[group, source], device_id=z_at(other), device_id_type=MESH)

    def whole_copy(other, source):
        return pltpu.make_async_remote_copy(pk.at[:, other], rx2.at[source], sz.at[0, other], rz.at[0, source], device_id=z_at(other), device_id_type=MESH)

    def forward(group):
        lo, hi = GROUPS[group]
        for slot in range(lo, hi):
            (own.wait if slot == 0 else first[slot].wait_recv)()
        lax.fori_loop(lo, hi, pack, 0)
        for other in Z_LOWER:
            @pl.when(other < z)
            def _():
                part_copy(group, other, z).start()

    forward(0)

    row = lax.broadcasted_iota(jnp.int32, (256, 256), 0)
    col = lax.broadcasted_iota(jnp.int32, (256, 256), 1)
    slot = (row >> 3) & 7
    back = jnp.where((slot & 1) == 1, (slot + 1) >> 1, 8 - (slot >> 1))
    source = ((y + 8 - back) & 7) * 2 + ((row >> 6) & 1)
    token = jnp.where(row < 128, source, 31 - source)
    target = ((row >> 2) & 1) * 128 + ((row >> 1) & 1) * 64 + token * 2 + (row & 1)
    perm[...] = jnp.where(col == target, 1.0, 0.0).astype(jnp.bfloat16)

    load.wait()

    def silu(step, carry):
        at = pl.ds(pl.multiple_of(step * 64, 64), 64)
        x = xf[at, :].astype(jnp.float32)
        sig = 1.0 / (1.0 + jnp.exp(-x))
        act[at, :] = (x * sig).astype(jnp.bfloat16)
        dsl[at, :] = sig * (1.0 + x * (1.0 - sig))
        return carry

    lax.fori_loop(0, 18, silu, 0)
    forward(1)
    lax.fori_loop(18, 36, silu, 0)
    forward(2)
    forward(3)
    for other in range(1, NZ):
        @pl.when(other > z)
        def _():
            pl.semaphore_wait(ready.at[other], 1)
            whole_copy(other, z).start()
    rx2[z] = pk[:, z]

    for other in range(NZ):
        @pl.when(other < z)
        def _():
            whole_copy(other, other).wait_recv()
            for group in range(len(GROUPS)):
                part_copy(group, other, other).wait_send()

        @pl.when(other > z)
        def _():
            for group in range(len(GROUPS)):
                part_copy(group, other, other).wait_recv()
            whole_copy(other, other).wait_send()
    for slot in range(1, NY):
        first[slot].wait_send()

    for r in range(8):
        low = rx2[r].astype(jnp.float32).reshape(64, 128)
        high = rx2[8 + r].astype(jnp.float32).reshape(64, 128)
        ts[r] = jnp.concatenate([low, high], axis=0).T
    for r in range(8):
        even = ts[r, pl.ds(0, 64, stride=2), :]
        odd = ts[r, pl.ds(1, 64, stride=2), :]
        left = jnp.concatenate([even, odd], axis=1).astype(jnp.bfloat16)
        moved = jnp.dot(left, perm[...], preferred_element_type=jnp.float32)
        os_[0, r * 64:(r + 1) * 64, :] = moved[:, 0:128]
        os_[1, r * 64:(r + 1) * 64, :] = moved[:, 128:256]
    top = rows == 0
    bottom = rows == 7
    for t in range(4):
        for g in range(5):
            for e in range(2):
                k0, k1, k2 = [os_[e, pl.ds(t * 16 + 3 * g + k, 8, stride=64), :] for k in range(3)]
                at = pl.ds(t * 16 + e, 8, stride=2)
                k1_64 = pltpu.roll(k1, 64, 1)
                k2_96 = pltpu.roll(k2, 96, 1)
                k0_32 = pltpu.roll(k0, 32, 1)
                if g > 0:
                    v0 = jnp.where(lane8 < 64, k0, jnp.where(lane8 < 96, k1_64, k0_32))
                    if g == 4:
                        v0 = jnp.where(bottom, 0.0, v0)
                    gt[3 * g, at, :] = v0
                if 0 < g < 4:
                    v1 = jnp.where(lane8 < 64, jnp.where(lane8 < 32, k0_32, pltpu.roll(k1, 96, 1)), jnp.where(lane8 < 96, pltpu.roll(k1, 32, 1), k2_96))
                    gt[3 * g + 1, at, :] = v1
                if g < 4:
                    v2 = jnp.where(lane8 < 32, k2_96, jnp.where(lane8 < 64, k1_64, k2))
                    if g == 0:
                        v2 = jnp.where(top, 0.0, v2)
                    gt[3 * g + 2, at, :] = v2

    place = lax.rem(lax.broadcasted_iota(jnp.int32, (16, 1152), 1), 96)
    for t in range(4):
        grid = jnp.concatenate([gt[v, 16 * t:16 * t + 16, :] for v in range(2, 13)], axis=1)
        for kh in range(3):
            for kw in range(3):
                off = 128 + (1 - kh) * 96 + 1 - kw
                block = (pltpu.roll(grid, 1408 - off, 1) if off % 1408 else grid)[:, 0:1152]
                if kw == 0:
                    block = jnp.where(place == 95, 0.0, block)
                if kw == 2:
                    block = jnp.where(place == 0, 0.0, block)
                at = (3 - t) * 144 + (kh * 3 + kw) * 16
                cols[at:at + 16, :] = block.astype(jnp.bfloat16)

    for c in range(3):
        lanes = slice(128 * c, 128 * c + 128)
        total = jnp.dot(cols[144:576, :], act[0:1152, lanes], preferred_element_type=jnp.float32)
        total = total + jnp.dot(cols[0:432, :], act[1152:2304, lanes], preferred_element_type=jnp.float32)
        total = total.reshape(54, 8, 128).astype(jnp.bfloat16)
        cut = min(max(USED_A - 54 * c, 0), 54)
        if cut > 0:
            sa[54 * c:54 * c + cut] = total[0:cut]
        if cut < 54:
            at = 54 * c + cut - USED_A
            sb[at:at + 54 - cut] = total[cut:54]
    sa[USED_A:ALL_A] = jnp.zeros((ALL_A - USED_A, 8, 128), jnp.bfloat16)

    def y_copy(source, target, ssem, rsem, d):
        return pltpu.make_async_remote_copy(source, target, ssem.at[d], rsem.at[d], device_id=y_dev(d)[1], device_id_type=MESH)

    def z_copy(source, target, ssem, rsem, d):
        return pltpu.make_async_remote_copy(source, target, ssem.at[d], rsem.at[d], device_id=z_dev(d)[1], device_id_type=MESH)

    first_a = {d: y_copy(sa.at[pl.ds(y_dev(d)[0] * OWN_A, OWN_A)], ra.at[d], s1a, r1a, d) for d in Y_ORDER}
    first_b = {d: z_copy(sb.at[pl.ds(z_dev(d)[0] * OWN_B, OWN_B)], rb.at[d], s1b, r1b, d) for d in Z_ORDER}
    for copy in [*first_a.values(), *first_b.values()]:
        copy.start()

    load_weight.wait()

    def backward(t):
        def one(step, carry):
            lanes = pl.ds(pl.multiple_of(step * 384, 128), 384)
            at = pl.ds(pl.multiple_of(t * 1152 + step * 384, 128), 384)
            pre = lax.dot_general(cols[(1 - t) * 144:(1 - t) * 144 + 432, lanes], weight[...], (((0,), (0,)), ((), ())), preferred_element_type=jnp.float32)
            grad_out[at, :] = (pre * dsl[at, :]).astype(jnp.bfloat16)
            return carry

        lax.fori_loop(0, 3, one, 0)

    backward(0)

    for copy in first_a.values():
        copy.wait_recv()
    part = sa[pl.ds(y * OWN_A, OWN_A)].astype(jnp.float32)
    for d in range(1, NY):
        part = part + ra[d].astype(jnp.float32)
    pa[...] = part
    for d in Z_ORDER:
        @pl.when(z_dev(d)[0] < OWN_A)
        def _():
            z_copy(pa.at[z_dev(d)[0]], qa.at[d], s2a, r2a, d).start()

    for copy in first_b.values():
        copy.wait_recv()
    part = sb[pl.ds(z * OWN_B, OWN_B)].astype(jnp.float32)
    for d in range(1, NZ):
        part = part + rb[d].astype(jnp.float32)
    pb[...] = part
    for d in Y_ORDER:
        @pl.when(y_dev(d)[0] < OWN_B)
        def _():
            y_copy(pb.at[y_dev(d)[0]], qb.at[d], s2b, r2b, d).start()

    mine_a = y * OWN_A + z
    mine_b = ALL_A + z * OWN_B + y

    @pl.when(z < OWN_A)
    def _():
        for d in range(1, NZ):
            z_copy(pa.at[0], qa.at[d], s2a, r2a, d).wait_recv()
        whole = pa[z]
        for d in range(1, NZ):
            whole = whole + qa[d]
        fin[mine_a] = (whole * scale).astype(jnp.bfloat16)
        for d in Z_ORDER:
            z_copy(fin.at[mine_a], fin.at[mine_a], s3a, r3a, d).start()

    @pl.when(y < OWN_B)
    def _():
        for d in range(1, NY):
            y_copy(pb.at[0], qb.at[d], s2b, r2b, d).wait_recv()
        whole = pb[y]
        for d in range(1, NY):
            whole = whole + qb[d]
        fin[mine_b] = (whole * scale).astype(jnp.bfloat16)
        for d in Y_ORDER:
            y_copy(fin.at[mine_b], fin.at[mine_b], s3b, r3b, d).start()

    for d in range(1, NZ):
        owner = lax.rem(z + NZ - d, NZ)

        @pl.when(owner < OWN_A)
        def _():
            piece = fin.at[y * OWN_A + owner]
            z_copy(piece, piece, s3a, r3a, d).wait_recv()
    block = fin.at[pl.ds(y * OWN_A, OWN_A)]
    last_a = {d: y_copy(block, block, s4a, r4a, d) for d in Y_ORDER}
    for copy in last_a.values():
        copy.start()

    for d in range(1, NY):
        owner = lax.rem(y + NY - d, NY)

        @pl.when(owner < OWN_B)
        def _():
            piece = fin.at[ALL_A + z * OWN_B + owner]
            y_copy(piece, piece, s3b, r3b, d).wait_recv()
    block = fin.at[pl.ds(ALL_A + z * OWN_B, OWN_B)]
    last_b = {d: z_copy(block, block, s4b, r4b, d) for d in Z_ORDER}
    for copy in last_b.values():
        copy.start()

    backward(1)

    for copy in [*first_a.values(), *first_b.values()]:
        copy.wait_send()
    for d in range(1, NZ):
        @pl.when(z_dev(d)[0] < OWN_A)
        def _():
            z_copy(pa.at[0], qa.at[d], s2a, r2a, d).wait_send()
    for d in range(1, NY):
        @pl.when(y_dev(d)[0] < OWN_B)
        def _():
            y_copy(pb.at[0], qb.at[d], s2b, r2b, d).wait_send()

    @pl.when(z < OWN_A)
    def _():
        for d in range(1, NZ):
            z_copy(fin.at[mine_a], fin.at[mine_a], s3a, r3a, d).wait_send()

    @pl.when(y < OWN_B)
    def _():
        for d in range(1, NY):
            y_copy(fin.at[mine_b], fin.at[mine_b], s3b, r3b, d).wait_send()

    for d, copy in last_a.items():
        copy.wait_send()
        landed = fin.at[pl.ds(lax.rem(y + NY - d, NY) * OWN_A, OWN_A)]
        y_copy(landed, landed, s4a, r4a, d).wait_recv()
    for d, copy in last_b.items():
        copy.wait_send()
        landed = fin.at[pl.ds(ALL_A + lax.rem(z + NZ - d, NZ) * OWN_B, OWN_B)]
        z_copy(landed, landed, s4b, r4b, d).wait_recv()
    b0 = 108 - USED_A
    sum_out[:, 0:128] = fin[0:54].astype(jnp.float32).reshape(432, 128)
    sum_out[0:432 - 8 * b0, 128:256] = fin[54:USED_A].astype(jnp.float32).reshape(432 - 8 * b0, 128)
    sum_out[432 - 8 * b0:432, 128:256] = fin[ALL_A:ALL_A + b0].astype(jnp.float32).reshape(8 * b0, 128)
    sum_out[:, 256:384] = fin[ALL_A + b0:ALL_A + b0 + 54].astype(jnp.float32).reshape(432, 128)


def shards(latent_grad, features, head_weight):
    frames, rows_here, width, channels = features.shape
    cells = frames * rows_here * width
    scale = 1.0 / math.sqrt(cells * NY * NZ)
    bf, f32 = jnp.bfloat16, jnp.float32
    dma = pltpu.SemaphoreType.DMA
    vmem = pl.BlockSpec(memory_space=pltpu.VMEM)
    hbm = pl.BlockSpec(memory_space=pl.ANY)
    grad, total = pl.pallas_call(
        lambda *refs: kernel(scale, *refs),
        out_shape=(
            pltpu.VMEM((cells, channels), bf),
            pltpu.VMEM((432, 384), f32),
        ),
        in_specs=[hbm, hbm, hbm],
        out_specs=(vmem, vmem),
        scratch_shapes=[
            pltpu.VMEM((432, 384), bf),
            pltpu.VMEM((cells, channels), bf),
            pltpu.VMEM((cells, channels), bf),
            pltpu.VMEM((cells, channels), f32),
            pltpu.VMEM((8, 1024), f32),
            pltpu.VMEM((NY, NZ, 8, 128), bf),
            pltpu.VMEM((NY, 8, 1408), bf),
            pltpu.VMEM((NZ, NY, 8, 128), bf),
            pltpu.VMEM((256, 256), bf),
            pltpu.VMEM((8, 128, 128), f32),
            pltpu.VMEM((2, 512, 128), f32),
            pltpu.VMEM((15, 64, 128), f32),
            pltpu.VMEM((576, 1152), bf),
            pltpu.VMEM((ALL_A, 8, 128), bf),
            pltpu.VMEM((NZ * OWN_B, 8, 128), bf),
            pltpu.VMEM((NY, OWN_A, 8, 128), bf),
            pltpu.VMEM((NZ, OWN_B, 8, 128), bf),
            pltpu.VMEM((OWN_A, 8, 128), f32),
            pltpu.VMEM((NZ, 8, 128), f32),
            pltpu.VMEM((OWN_B, 8, 128), f32),
            pltpu.VMEM((NY, 8, 128), f32),
            pltpu.VMEM((ALL_A + NZ * OWN_B, 8, 128), bf),
            dma((3,)), pltpu.SemaphoreType.REGULAR((NZ,)),
            dma((NY,)), dma((NY,)), dma((len(GROUPS), NZ)), dma((len(GROUPS), NZ)),
            dma((NY,)), dma((NY,)), dma((NZ,)), dma((NZ,)),
            dma((NZ,)), dma((NZ,)), dma((NY,)), dma((NY,)),
            dma((NZ,)), dma((NZ,)), dma((NY,)), dma((NY,)),
            dma((NY,)), dma((NY,)), dma((NZ,)), dma((NZ,)),
        ],
        compiler_params=pltpu.CompilerParams(collective_id=0, has_side_effects=True),
        name="encoder_head_backward",
    )(latent_grad.T, features.reshape(cells, channels), head_weight)
    return grad.reshape(features.shape), total


def solution(mesh):
    return jax.shard_map(
        shards,
        mesh=mesh,
        in_specs=(P(("dp", "tm"), "rows"), P(("dp", "tm"), "rows", None, None), P()),
        out_specs=(P(("dp", "tm"), "rows", None, None), P("dp", None)),
        check_vma=False,
    )
```

```python
import math

import jax
import jax.numpy as jnp
from jax import lax
from jax.experimental import pallas as pl
from jax.experimental.pallas import tpu as pltpu
from jax.sharding import PartitionSpec as P

NY = 8
NZ = 16
OWN_A = 14
OWN_B = 4
ALL_A = 112
USED_A = 98
MESH = pl.DeviceIdType.MESH
Y_ORDER = (4, 3, 5, 2, 6, 1, 7)
SLOTS = (0, 1, 7, 2, 6, 3, 5, 4)
Z_LOWER = (7, 6, 8, 5, 9, 4, 10, 3, 11, 2, 12, 1, 13, 0, 14)
GROUPS = 2
Z_ORDER = (8, 7, 9, 6, 10, 5, 11, 4, 12, 3, 13, 2, 14, 1, 15)


def kernel(scale, lat_hbm, feat, weight_hbm, grad_out, sum_out, weight, xf, act, dsl, lp, pk, rx1, rx2, perm, ts, os_, gt, cols, sa, sb, ra, rb, pa, qa, pb, qb, fin, in_sem, ready, sy, ry, sz, rz, s1a, r1a, s1b, r1b, s2a, r2a, s2b, r2b, s3a, r3a, s3b, r3b, s4a, r4a, s4b, r4b):
    tm = lax.axis_index("tm")
    rows = lax.axis_index("rows")
    y = lax.div(tm, 2)
    zh = lax.rem(tm, 2)
    z = zh * 8 + rows

    def y_dev(d):
        other = lax.rem(y + d, NY)
        return other, {"tm": other * 2 + zh}

    def z_dev(d):
        other = lax.rem(z + d, NZ)
        return other, {"tm": y * 2 + lax.div(other, 8), "rows": lax.rem(other, 8)}

    def z_at(other):
        return {"tm": y * 2 + other // 8, "rows": other % 8}

    def window(other):
        first_tile = jnp.minimum(lax.div(9 * other, 2), 28)
        return lat_hbm.at[:, pl.ds(pl.multiple_of(first_tile * 128, 128), 1024)]

    own = pltpu.make_async_copy(window(y), rx1.at[0, :, 0:1024], in_sem.at[0])
    own.start()
    load = pltpu.make_async_copy(feat, xf, in_sem.at[1])
    load.start()
    load_weight = pltpu.make_async_copy(weight_hbm, weight, in_sem.at[2])
    load_weight.start()

    barrier = pltpu.get_barrier_semaphore()
    for d in range(1, NY):
        pl.semaphore_signal(barrier, inc=1, device_id=y_dev(d)[1], device_id_type=MESH)
    for other in range(1, NZ):
        @pl.when(other > z)
        def _():
            pl.semaphore_signal(barrier, inc=1, device_id=z_at(other), device_id_type=MESH)
    rx1[:, :, 1024:1408] = jnp.zeros((NY, 8, 384), jnp.bfloat16)
    lp[:, :, 0:128] = jnp.zeros((4, 8, 128), jnp.float32)
    pl.semaphore_wait(barrier, NY - 1 + z)

    first = [None] * NY
    for slot in range(1, NY):
        other, dev = y_dev(SLOTS[slot])
        copy = pltpu.make_async_remote_copy(window(other), rx1.at[slot, :, 0:1024], sy.at[slot], ry.at[slot], device_id=dev, device_id_type=MESH)
        copy.start()
        first[slot] = copy
    for other in range(NZ - 1):
        @pl.when(other < z)
        def _():
            pl.semaphore_signal(ready.at[z], inc=1, device_id=z_at(other), device_id_type=MESH)

    lane8 = lax.broadcasted_iota(jnp.int32, (8, 128), 1)
    base = pl.multiple_of(jnp.where(y == NY - 1, 384, 0), 128)
    odd = lax.rem(y, 2) == 1

    def pack(group):
        for s in range(4):
            tiles = [rx1[4 * group + s, :, pl.ds(base + 128 * j, 128)].astype(jnp.float32) for j in range(8)]
            turned = [pltpu.roll(tile, 64, 1) for tile in tiles]
            for j in range(7):
                lp[s, :, 128 * j + 128:128 * j + 256] = jnp.where(odd, jnp.where(lane8 < 64, turned[j], turned[j + 1]), tiles[j])
        for zd in range(NZ):
            values = [None] * 3
            for n in range(16):
                s, tt = n // 4, n % 4
                start = 128 + 288 * (zd // 8) + 144 * tt + 18 * (zd % 8) - 3
                move = 24 * n - start
                for v in range(start // 128, (start + 23) // 128 + 1):
                    tile = lp[s, :, 128 * v:128 * v + 128]
                    shift = move % 128
                    tile = pltpu.roll(tile, shift, 1) if shift else tile
                    lo = max(24 * n, 128 * v + move)
                    hi = min(24 * n + 24, 128 * v + 128 + move)
                    for j in range(lo // 128, (hi - 1) // 128 + 1):
                        at = max(lo - 128 * j, 0)
                        values[j] = tile if at == 0 else jnp.where(lane8 < at, values[j], tile)
            for j in range(3):
                pk[3 * group + j, zd] = values[j].astype(jnp.bfloat16)

    def part_copy(group, other, source):
        lo, hi = 3 * group, 3 * group + 3
        return pltpu.make_async_remote_copy(pk.at[lo:hi, other], rx2.at[source, lo:hi], sz.at[group, other], rz.at[group, source], device_id=z_at(other), device_id_type=MESH)

    def whole_copy(other, source):
        return pltpu.make_async_remote_copy(pk.at[:, other], rx2.at[source], sz.at[0, other], rz.at[0, source], device_id=z_at(other), device_id_type=MESH)

    def forward(group):
        for slot in range(4 * group, 4 * group + 4):
            (own.wait if slot == 0 else first[slot].wait_recv)()
        pack(group)
        for other in Z_LOWER:
            @pl.when(other < z)
            def _():
                part_copy(group, other, z).start()

    row = lax.broadcasted_iota(jnp.int32, (256, 256), 0)
    col = lax.broadcasted_iota(jnp.int32, (256, 256), 1)
    slot = (row >> 3) & 7
    back = jnp.where((slot & 1) == 1, (slot + 1) >> 1, 8 - (slot >> 1))
    source = ((y + 8 - back) & 7) * 2 + ((row >> 6) & 1)
    token = jnp.where(row < 128, 15 - source, source + 16)
    target = ((row >> 2) & 1) * 128 + ((row >> 1) & 1) * 64 + token * 2 + (row & 1)
    perm[...] = jnp.where(col == target, 1.0, 0.0).astype(jnp.bfloat16)

    forward(0)
    forward(1)
    load.wait()

    def silu(step, carry):
        at = pl.ds(pl.multiple_of(step * 64, 64), 64)
        x = xf[at, :].astype(jnp.float32)
        sig = 1.0 / (1.0 + jnp.exp(-x))
        act[at, :] = (x * sig).astype(jnp.bfloat16)
        dsl[at, :] = sig * (1.0 + x * (1.0 - sig))
        return carry

    lax.fori_loop(0, 36, silu, 0)
    for other in range(1, NZ):
        @pl.when(other > z)
        def _():
            pl.semaphore_wait(ready.at[other], 1)
            whole_copy(other, z).start()
    rx2[z] = pk[:, z]

    for other in range(NZ):
        @pl.when(other < z)
        def _():
            whole_copy(other, other).wait_recv()
            for group in range(GROUPS):
                part_copy(group, other, other).wait_send()

        @pl.when(other > z)
        def _():
            for group in range(GROUPS):
                part_copy(group, other, other).wait_recv()
            whole_copy(other, other).wait_send()
    for slot in range(1, NY):
        first[slot].wait_send()

    def unpack(zs):
        parts = []
        for group in range(GROUPS):
            t0, t1, t2 = [rx2[zs, 3 * group + j].astype(jnp.float32) for j in range(3)]
            parts.append(t0)
            parts.append(jnp.where(lane8 < 32, pltpu.roll(t0, 32, 1), pltpu.roll(t1, 32, 1)))
            parts.append(jnp.where(lane8 < 64, pltpu.roll(t1, 64, 1), pltpu.roll(t2, 64, 1)))
            parts.append(pltpu.roll(t2, 96, 1))
        return parts

    for r in range(8):
        ts[r] = jnp.concatenate(unpack(r) + unpack(8 + r), axis=0).T
    for r in range(8):
        even = ts[r, pl.ds(0, 48, stride=2), :]
        odds = ts[r, pl.ds(1, 48, stride=2), :]
        left = jnp.concatenate([even, odds], axis=1).astype(jnp.bfloat16)
        moved = jnp.dot(left, perm[...], preferred_element_type=jnp.float32)
        os_[0, r * 48:(r + 1) * 48, :] = moved[:, 0:128]
        os_[1, r * 48:(r + 1) * 48, :] = moved[:, 128:256]
    top = rows == 0
    bottom = rows == 7
    for t in range(4):
        for g in range(4):
            for e in range(2):
                k0, k1, k2 = [os_[e, pl.ds(t * 12 + 3 * g + k, 8, stride=48), :] for k in range(3)]
                at = pl.ds(t * 16 + e, 8, stride=2)
                k1_64 = pltpu.roll(k1, 64, 1)
                k2_96 = pltpu.roll(k2, 96, 1)
                k0_32 = pltpu.roll(k0, 32, 1)
                v0 = jnp.where(lane8 < 64, k0, jnp.where(lane8 < 96, k1_64, k0_32))
                v1 = jnp.where(lane8 < 64, jnp.where(lane8 < 32, k0_32, pltpu.roll(k1, 96, 1)), jnp.where(lane8 < 96, pltpu.roll(k1, 32, 1), k2_96))
                v2 = jnp.where(lane8 < 32, k2_96, jnp.where(lane8 < 64, k1_64, k2))
                if g == 0:
                    v0 = jnp.where(top, 0.0, v0)
                    v1 = jnp.where(jnp.logical_and(top, lane8 < 64), 0.0, v1)
                if g == 3:
                    v1 = jnp.where(jnp.logical_and(bottom, lane8 >= 64), 0.0, v1)
                    v2 = jnp.where(bottom, 0.0, v2)
                gt[3 * g, at, :] = v0
                gt[3 * g + 1, at, :] = v1
                gt[3 * g + 2, at, :] = v2

    place = lax.rem(lax.broadcasted_iota(jnp.int32, (16, 1152), 1), 96)
    for t in range(4):
        grid = jnp.concatenate([gt[v, 16 * t:16 * t + 16, :] for v in range(12)], axis=1)
        for kh in range(3):
            for kw in range(3):
                off = 192 + (1 - kh) * 96 + 1 - kw
                block = pltpu.roll(grid, 1536 - off, 1)[:, 0:1152]
                if kw == 0:
                    block = jnp.where(place == 95, 0.0, block)
                if kw == 2:
                    block = jnp.where(place == 0, 0.0, block)
                at = (3 - t) * 144 + (kh * 3 + kw) * 16
                cols[at:at + 16, :] = block.astype(jnp.bfloat16)

    for c in range(3):
        lanes = slice(128 * c, 128 * c + 128)
        total = jnp.dot(cols[144:576, :], act[0:1152, lanes], preferred_element_type=jnp.float32)
        total = total + jnp.dot(cols[0:432, :], act[1152:2304, lanes], preferred_element_type=jnp.float32)
        total = total.reshape(54, 8, 128).astype(jnp.bfloat16)
        cut = min(max(USED_A - 54 * c, 0), 54)
        if cut > 0:
            sa[54 * c:54 * c + cut] = total[0:cut]
        if cut < 54:
            at = 54 * c + cut - USED_A
            sb[at:at + 54 - cut] = total[cut:54]
    sa[USED_A:ALL_A] = jnp.zeros((ALL_A - USED_A, 8, 128), jnp.bfloat16)

    def y_copy(source, target, ssem, rsem, d):
        return pltpu.make_async_remote_copy(source, target, ssem.at[d], rsem.at[d], device_id=y_dev(d)[1], device_id_type=MESH)

    def z_copy(source, target, ssem, rsem, d):
        return pltpu.make_async_remote_copy(source, target, ssem.at[d], rsem.at[d], device_id=z_dev(d)[1], device_id_type=MESH)

    first_a = {d: y_copy(sa.at[pl.ds(y_dev(d)[0] * OWN_A, OWN_A)], ra.at[d], s1a, r1a, d) for d in Y_ORDER}
    first_b = {d: z_copy(sb.at[pl.ds(z_dev(d)[0] * OWN_B, OWN_B)], rb.at[d], s1b, r1b, d) for d in Z_ORDER}
    for copy in [*first_a.values(), *first_b.values()]:
        copy.start()

    load_weight.wait()

    def backward(t):
        def one(step, carry):
            lanes = pl.ds(pl.multiple_of(step * 384, 128), 384)
            at = pl.ds(pl.multiple_of(t * 1152 + step * 384, 128), 384)
            pre = lax.dot_general(cols[(1 - t) * 144:(1 - t) * 144 + 432, lanes], weight[...], (((0,), (0,)), ((), ())), preferred_element_type=jnp.float32)
            grad_out[at, :] = (pre * dsl[at, :]).astype(jnp.bfloat16)
            return carry

        lax.fori_loop(0, 3, one, 0)

    backward(0)

    for copy in first_a.values():
        copy.wait_recv()
    part = sa[pl.ds(y * OWN_A, OWN_A)].astype(jnp.float32)
    for d in range(1, NY):
        part = part + ra[d].astype(jnp.float32)
    pa[...] = part
    for d in Z_ORDER:
        @pl.when(z_dev(d)[0] < OWN_A)
        def _():
            z_copy(pa.at[z_dev(d)[0]], qa.at[d], s2a, r2a, d).start()

    for copy in first_b.values():
        copy.wait_recv()
    part = sb[pl.ds(z * OWN_B, OWN_B)].astype(jnp.float32)
    for d in range(1, NZ):
        part = part + rb[d].astype(jnp.float32)
    pb[...] = part
    for d in Y_ORDER:
        @pl.when(y_dev(d)[0] < OWN_B)
        def _():
            y_copy(pb.at[y_dev(d)[0]], qb.at[d], s2b, r2b, d).start()

    mine_a = y * OWN_A + z
    mine_b = ALL_A + z * OWN_B + y

    @pl.when(y < OWN_B)
    def _():
        for d in range(1, NY):
            y_copy(pb.at[0], qb.at[d], s2b, r2b, d).wait_recv()
        whole = pb[y]
        for d in range(1, NY):
            whole = whole + qb[d]
        fin[mine_b] = (whole * scale).astype(jnp.bfloat16)
        for d in Y_ORDER:
            y_copy(fin.at[mine_b], fin.at[mine_b], s3b, r3b, d).start()

    @pl.when(z < OWN_A)
    def _():
        for d in range(1, NZ):
            z_copy(pa.at[0], qa.at[d], s2a, r2a, d).wait_recv()
        whole = pa[z]
        for d in range(1, NZ):
            whole = whole + qa[d]
        fin[mine_a] = (whole * scale).astype(jnp.bfloat16)
        for d in Z_ORDER:
            z_copy(fin.at[mine_a], fin.at[mine_a], s3a, r3a, d).start()

    for d in range(1, NY):
        owner = lax.rem(y + NY - d, NY)

        @pl.when(owner < OWN_B)
        def _():
            piece = fin.at[ALL_A + z * OWN_B + owner]
            y_copy(piece, piece, s3b, r3b, d).wait_recv()
    block = fin.at[pl.ds(ALL_A + z * OWN_B, OWN_B)]
    last_b = {d: z_copy(block, block, s4b, r4b, d) for d in Z_ORDER}
    for copy in last_b.values():
        copy.start()

    for d in range(1, NZ):
        owner = lax.rem(z + NZ - d, NZ)

        @pl.when(owner < OWN_A)
        def _():
            piece = fin.at[y * OWN_A + owner]
            z_copy(piece, piece, s3a, r3a, d).wait_recv()
    block = fin.at[pl.ds(y * OWN_A, OWN_A)]
    last_a = {d: y_copy(block, block, s4a, r4a, d) for d in Y_ORDER}
    for copy in last_a.values():
        copy.start()

    backward(1)

    for copy in [*first_a.values(), *first_b.values()]:
        copy.wait_send()
    for d in range(1, NZ):
        @pl.when(z_dev(d)[0] < OWN_A)
        def _():
            z_copy(pa.at[0], qa.at[d], s2a, r2a, d).wait_send()
    for d in range(1, NY):
        @pl.when(y_dev(d)[0] < OWN_B)
        def _():
            y_copy(pb.at[0], qb.at[d], s2b, r2b, d).wait_send()

    @pl.when(z < OWN_A)
    def _():
        for d in range(1, NZ):
            z_copy(fin.at[mine_a], fin.at[mine_a], s3a, r3a, d).wait_send()

    @pl.when(y < OWN_B)
    def _():
        for d in range(1, NY):
            y_copy(fin.at[mine_b], fin.at[mine_b], s3b, r3b, d).wait_send()

    for d, copy in last_a.items():
        copy.wait_send()
        landed = fin.at[pl.ds(lax.rem(y + NY - d, NY) * OWN_A, OWN_A)]
        y_copy(landed, landed, s4a, r4a, d).wait_recv()
    for d, copy in last_b.items():
        copy.wait_send()
        landed = fin.at[pl.ds(ALL_A + lax.rem(z + NZ - d, NZ) * OWN_B, OWN_B)]
        z_copy(landed, landed, s4b, r4b, d).wait_recv()
    b0 = 108 - USED_A
    sum_out[:, 0:128] = fin[0:54].astype(jnp.float32).reshape(432, 128)
    sum_out[0:432 - 8 * b0, 128:256] = fin[54:USED_A].astype(jnp.float32).reshape(432 - 8 * b0, 128)
    sum_out[432 - 8 * b0:432, 128:256] = fin[ALL_A:ALL_A + b0].astype(jnp.float32).reshape(8 * b0, 128)
    sum_out[:, 256:384] = fin[ALL_A + b0:ALL_A + b0 + 54].astype(jnp.float32).reshape(432, 128)


def shards(latent_grad, features, head_weight):
    frames, rows_here, width, channels = features.shape
    cells = frames * rows_here * width
    scale = 1.0 / math.sqrt(cells * NY * NZ)
    bf, f32 = jnp.bfloat16, jnp.float32
    dma = pltpu.SemaphoreType.DMA
    vmem = pl.BlockSpec(memory_space=pltpu.VMEM)
    hbm = pl.BlockSpec(memory_space=pl.ANY)
    grad, total = pl.pallas_call(
        lambda *refs: kernel(scale, *refs),
        out_shape=(
            pltpu.VMEM((cells, channels), bf),
            pltpu.VMEM((432, 384), f32),
        ),
        in_specs=[hbm, hbm, hbm],
        out_specs=(vmem, vmem),
        scratch_shapes=[
            pltpu.VMEM((432, 384), bf),
            pltpu.VMEM((cells, channels), bf),
            pltpu.VMEM((cells, channels), bf),
            pltpu.VMEM((cells, channels), f32),
            pltpu.VMEM((4, 8, 1024), f32),
            pltpu.VMEM((3 * GROUPS, NZ, 8, 128), bf),
            pltpu.VMEM((NY, 8, 1408), bf),
            pltpu.VMEM((NZ, 3 * GROUPS, 8, 128), bf),
            pltpu.VMEM((256, 256), bf),
            pltpu.VMEM((8, 128, 128), f32),
            pltpu.VMEM((2, 384, 128), f32),
            pltpu.VMEM((12, 64, 128), f32),
            pltpu.VMEM((576, 1152), bf),
            pltpu.VMEM((ALL_A, 8, 128), bf),
            pltpu.VMEM((NZ * OWN_B, 8, 128), bf),
            pltpu.VMEM((NY, OWN_A, 8, 128), bf),
            pltpu.VMEM((NZ, OWN_B, 8, 128), bf),
            pltpu.VMEM((OWN_A, 8, 128), f32),
            pltpu.VMEM((NZ, 8, 128), f32),
            pltpu.VMEM((OWN_B, 8, 128), f32),
            pltpu.VMEM((NY, 8, 128), f32),
            pltpu.VMEM((ALL_A + NZ * OWN_B, 8, 128), bf),
            dma((3,)), pltpu.SemaphoreType.REGULAR((NZ,)),
            dma((NY,)), dma((NY,)), dma((GROUPS, NZ)), dma((GROUPS, NZ)),
            dma((NY,)), dma((NY,)), dma((NZ,)), dma((NZ,)),
            dma((NZ,)), dma((NZ,)), dma((NY,)), dma((NY,)),
            dma((NZ,)), dma((NZ,)), dma((NY,)), dma((NY,)),
            dma((NY,)), dma((NY,)), dma((NZ,)), dma((NZ,)),
        ],
        compiler_params=pltpu.CompilerParams(collective_id=0, has_side_effects=True),
        name="encoder_head_backward",
    )(latent_grad.T, features.reshape(cells, channels), head_weight)
    return grad.reshape(features.shape), total


def solution(mesh):
    return jax.shard_map(
        shards,
        mesh=mesh,
        in_specs=(P(("dp", "tm"), "rows"), P(("dp", "tm"), "rows", None, None), P()),
        out_specs=(P(("dp", "tm"), "rows", None, None), P("dp", None)),
        check_vma=False,
    )
```

```python
import math

import jax
import jax.numpy as jnp
from jax import lax
from jax.experimental import pallas as pl
from jax.experimental.pallas import tpu as pltpu
from jax.sharding import PartitionSpec as P

NY = 8
NZ = 16
OWN_A = 15
OWN_B = 3
ALL_A = 120
USED_A = 114
MESH = pl.DeviceIdType.MESH
Y_ORDER = (4, 3, 5, 2, 6, 1, 7)
SLOTS = (0, 1, 7, 2, 6, 3, 5, 4)
Z_LOWER = (7, 6, 8, 5, 9, 4, 10, 3, 11, 2, 12, 1, 13, 0, 14)
GROUPS = 2
Y_NEAR = (1, 7, 2, 6, 3, 5, 4)
Z_NEAR = (1, 15, 2, 14, 3, 13, 4, 12, 5, 11, 6, 10, 7, 9, 8)
Z_ORDER = (8, 7, 9, 6, 10, 5, 11, 4, 12, 3, 13, 2, 14, 1, 15)


def kernel(scale, lat_hbm, feat, weight_hbm, grad_out, sum_out, weight, xf, act, dsl, lp, pk, rx1, rx2, perm, ts, os_, gt, cols, sa, sb, ra, rb, pa, qa, pb, qb, fin, in_sem, ready, sy, ry, sz, rz, s1a, r1a, s1b, r1b, s2a, r2a, s2b, r2b, s3a, r3a, s3b, r3b, s4a, r4a, s4b, r4b):
    tm = lax.axis_index("tm")
    rows = lax.axis_index("rows")
    y = lax.div(tm, 2)
    zh = lax.rem(tm, 2)
    z = zh * 8 + rows

    def y_dev(d):
        other = lax.rem(y + d, NY)
        return other, {"tm": other * 2 + zh}

    def z_dev(d):
        other = lax.rem(z + d, NZ)
        return other, {"tm": y * 2 + lax.div(other, 8), "rows": lax.rem(other, 8)}

    def z_at(other):
        return {"tm": y * 2 + other // 8, "rows": other % 8}

    def window(other):
        first_tile = jnp.minimum(lax.div(9 * other, 2), 28)
        return lat_hbm.at[:, pl.ds(pl.multiple_of(first_tile * 128, 128), 1024)]

    own = pltpu.make_async_copy(window(y), rx1.at[0, :, 0:1024], in_sem.at[0])
    own.start()
    load = pltpu.make_async_copy(feat, xf, in_sem.at[1])
    load.start()
    load_weight = pltpu.make_async_copy(weight_hbm, weight, in_sem.at[2])
    load_weight.start()

    barrier = pltpu.get_barrier_semaphore()
    for d in range(1, NY):
        pl.semaphore_signal(barrier, inc=1, device_id=y_dev(d)[1], device_id_type=MESH)
    for other in range(1, NZ):
        @pl.when(other > z)
        def _():
            pl.semaphore_signal(barrier, inc=1, device_id=z_at(other), device_id_type=MESH)
    rx1[:, :, 1024:1408] = jnp.zeros((NY, 8, 384), jnp.bfloat16)
    lp[:, :, 0:128] = jnp.zeros((4, 8, 128), jnp.float32)
    pl.semaphore_wait(barrier, NY - 1 + z)

    first = [None] * NY
    for slot in range(1, NY):
        other, dev = y_dev(SLOTS[slot])
        copy = pltpu.make_async_remote_copy(window(other), rx1.at[slot, :, 0:1024], sy.at[slot], ry.at[slot], device_id=dev, device_id_type=MESH)
        copy.start()
        first[slot] = copy
    for other in range(NZ - 1):
        @pl.when(other < z)
        def _():
            pl.semaphore_signal(ready.at[z], inc=1, device_id=z_at(other), device_id_type=MESH)

    lane8 = lax.broadcasted_iota(jnp.int32, (8, 128), 1)
    base = pl.multiple_of(jnp.where(y == NY - 1, 384, 0), 128)
    odd = lax.rem(y, 2) == 1

    def pack(group):
        for s in range(4):
            tiles = [rx1[4 * group + s, :, pl.ds(base + 128 * j, 128)].astype(jnp.float32) for j in range(8)]
            turned = [pltpu.roll(tile, 64, 1) for tile in tiles]
            for j in range(7):
                lp[s, :, 128 * j + 128:128 * j + 256] = jnp.where(odd, jnp.where(lane8 < 64, turned[j], turned[j + 1]), tiles[j])
        for zd in range(NZ):
            values = [None] * 3
            for n in range(16):
                s, tt = n // 4, n % 4
                start = 128 + 288 * (zd // 8) + 144 * tt + 18 * (zd % 8) - 3
                move = 24 * n - start
                for v in range(start // 128, (start + 23) // 128 + 1):
                    tile = lp[s, :, 128 * v:128 * v + 128]
                    shift = move % 128
                    tile = pltpu.roll(tile, shift, 1) if shift else tile
                    lo = max(24 * n, 128 * v + move)
                    hi = min(24 * n + 24, 128 * v + 128 + move)
                    for j in range(lo // 128, (hi - 1) // 128 + 1):
                        at = max(lo - 128 * j, 0)
                        values[j] = tile if at == 0 else jnp.where(lane8 < at, values[j], tile)
            for j in range(3):
                pk[3 * group + j, zd] = values[j].astype(jnp.bfloat16)

    def part_copy(group, other, source):
        lo, hi = 3 * group, 3 * group + 3
        return pltpu.make_async_remote_copy(pk.at[lo:hi, other], rx2.at[source, lo:hi], sz.at[group, other], rz.at[group, source], device_id=z_at(other), device_id_type=MESH)

    def whole_copy(other, source):
        return pltpu.make_async_remote_copy(pk.at[:, other], rx2.at[source], sz.at[0, other], rz.at[0, source], device_id=z_at(other), device_id_type=MESH)

    def forward(group):
        for slot in range(4 * group, 4 * group + 4):
            (own.wait if slot == 0 else first[slot].wait_recv)()
        pack(group)
        for other in Z_LOWER:
            @pl.when(other < z)
            def _():
                part_copy(group, other, z).start()

    row = lax.broadcasted_iota(jnp.int32, (256, 256), 0)
    col = lax.broadcasted_iota(jnp.int32, (256, 256), 1)
    slot = (row >> 3) & 7
    back = jnp.where((slot & 1) == 1, (slot + 1) >> 1, 8 - (slot >> 1))
    source = ((y + 8 - back) & 7) * 2 + ((row >> 6) & 1)
    token = jnp.where(row < 128, 15 - source, source + 16)
    target = ((row >> 2) & 1) * 128 + ((row >> 1) & 1) * 64 + token * 2 + (row & 1)
    perm[...] = jnp.where(col == target, 1.0, 0.0).astype(jnp.bfloat16)

    forward(0)
    forward(1)
    load.wait()

    def silu(step, carry):
        at = pl.ds(pl.multiple_of(step * 64, 64), 64)
        x = xf[at, :].astype(jnp.float32)
        sig = 1.0 / (1.0 + jnp.exp(-x))
        act[at, :] = (x * sig).astype(jnp.bfloat16)
        dsl[at, :] = sig * (1.0 + x * (1.0 - sig))
        return carry

    lax.fori_loop(0, 36, silu, 0)
    for other in range(1, NZ):
        @pl.when(other > z)
        def _():
            pl.semaphore_wait(ready.at[other], 1)
            whole_copy(other, z).start()
    rx2[z] = pk[:, z]

    for other in range(NZ):
        @pl.when(other < z)
        def _():
            whole_copy(other, other).wait_recv()
            for group in range(GROUPS):
                part_copy(group, other, other).wait_send()

        @pl.when(other > z)
        def _():
            for group in range(GROUPS):
                part_copy(group, other, other).wait_recv()
            whole_copy(other, other).wait_send()
    for slot in range(1, NY):
        first[slot].wait_send()

    def unpack(zs):
        parts = []
        for group in range(GROUPS):
            t0, t1, t2 = [rx2[zs, 3 * group + j].astype(jnp.float32) for j in range(3)]
            parts.append(t0)
            parts.append(jnp.where(lane8 < 32, pltpu.roll(t0, 32, 1), pltpu.roll(t1, 32, 1)))
            parts.append(jnp.where(lane8 < 64, pltpu.roll(t1, 64, 1), pltpu.roll(t2, 64, 1)))
            parts.append(pltpu.roll(t2, 96, 1))
        return parts

    for r in range(8):
        ts[r] = jnp.concatenate(unpack(r) + unpack(8 + r), axis=0).T
    for r in range(8):
        even = ts[r, pl.ds(0, 48, stride=2), :]
        odds = ts[r, pl.ds(1, 48, stride=2), :]
        left = jnp.concatenate([even, odds], axis=1).astype(jnp.bfloat16)
        moved = jnp.dot(left, perm[...], preferred_element_type=jnp.float32)
        os_[0, r * 48:(r + 1) * 48, :] = moved[:, 0:128]
        os_[1, r * 48:(r + 1) * 48, :] = moved[:, 128:256]
    top = rows == 0
    bottom = rows == 7
    for t in range(4):
        for g in range(4):
            for e in range(2):
                k0, k1, k2 = [os_[e, pl.ds(t * 12 + 3 * g + k, 8, stride=48), :] for k in range(3)]
                at = pl.ds(t * 16 + e, 8, stride=2)
                k1_64 = pltpu.roll(k1, 64, 1)
                k2_96 = pltpu.roll(k2, 96, 1)
                k0_32 = pltpu.roll(k0, 32, 1)
                v0 = jnp.where(lane8 < 64, k0, jnp.where(lane8 < 96, k1_64, k0_32))
                v1 = jnp.where(lane8 < 64, jnp.where(lane8 < 32, k0_32, pltpu.roll(k1, 96, 1)), jnp.where(lane8 < 96, pltpu.roll(k1, 32, 1), k2_96))
                v2 = jnp.where(lane8 < 32, k2_96, jnp.where(lane8 < 64, k1_64, k2))
                if g == 0:
                    v0 = jnp.where(top, 0.0, v0)
                    v1 = jnp.where(jnp.logical_and(top, lane8 < 64), 0.0, v1)
                if g == 3:
                    v1 = jnp.where(jnp.logical_and(bottom, lane8 >= 64), 0.0, v1)
                    v2 = jnp.where(bottom, 0.0, v2)
                gt[3 * g, at, :] = v0
                gt[3 * g + 1, at, :] = v1
                gt[3 * g + 2, at, :] = v2

    place = lax.rem(lax.broadcasted_iota(jnp.int32, (16, 1152), 1), 96)
    for t in range(4):
        grid = jnp.concatenate([gt[v, 16 * t:16 * t + 16, :] for v in range(12)], axis=1)
        for kh in range(3):
            for kw in range(3):
                off = 192 + (1 - kh) * 96 + 1 - kw
                block = pltpu.roll(grid, 1536 - off, 1)[:, 0:1152]
                if kw == 0:
                    block = jnp.where(place == 95, 0.0, block)
                if kw == 2:
                    block = jnp.where(place == 0, 0.0, block)
                at = (3 - t) * 144 + (kh * 3 + kw) * 16
                cols[at:at + 16, :] = block.astype(jnp.bfloat16)

    def y_copy(source, target, ssem, rsem, d):
        return pltpu.make_async_remote_copy(source, target, ssem.at[d], rsem.at[d], device_id=y_dev(d)[1], device_id_type=MESH)

    def z_copy(source, target, ssem, rsem, d):
        return pltpu.make_async_remote_copy(source, target, ssem.at[d], rsem.at[d], device_id=z_dev(d)[1], device_id_type=MESH)

    def weight_part(c):
        lanes = slice(128 * c, 128 * c + 128)
        total = jnp.dot(cols[144:576, :], act[0:1152, lanes], preferred_element_type=jnp.float32)
        total = total + jnp.dot(cols[0:432, :], act[1152:2304, lanes], preferred_element_type=jnp.float32)
        total = total.reshape(54, 8, 128).astype(jnp.bfloat16)
        cut = min(max(USED_A - 54 * c, 0), 54)
        if cut > 0:
            sa[54 * c:54 * c + cut] = total[0:cut]
        if cut < 54:
            at = 54 * c + cut - USED_A
            sb[at:at + 54 - cut] = total[cut:54]

    weight_part(2)
    first_b = {d: z_copy(sb.at[pl.ds(z_dev(d)[0] * OWN_B, OWN_B)], rb.at[d], s1b, r1b, d) for d in Z_ORDER}
    for copy in first_b.values():
        copy.start()
    weight_part(1)
    weight_part(0)
    sa[USED_A:ALL_A] = jnp.zeros((ALL_A - USED_A, 8, 128), jnp.bfloat16)
    first_a = {d: y_copy(sa.at[pl.ds(y_dev(d)[0] * OWN_A, OWN_A)], ra.at[d], s1a, r1a, d) for d in Y_ORDER}
    for copy in first_a.values():
        copy.start()

    load_weight.wait()

    def backward(t):
        def one(step, carry):
            lanes = pl.ds(pl.multiple_of(step * 384, 128), 384)
            at = pl.ds(pl.multiple_of(t * 1152 + step * 384, 128), 384)
            pre = lax.dot_general(cols[(1 - t) * 144:(1 - t) * 144 + 432, lanes], weight[...], (((0,), (0,)), ((), ())), preferred_element_type=jnp.float32)
            grad_out[at, :] = (pre * dsl[at, :]).astype(jnp.bfloat16)
            return carry

        lax.fori_loop(0, 3, one, 0)

    backward(0)

    for copy in first_a.values():
        copy.wait_recv()
    part = sa[pl.ds(y * OWN_A, OWN_A)].astype(jnp.float32)
    for d in range(1, NY):
        part = part + ra[d].astype(jnp.float32)
    pa[...] = part
    for d in Z_ORDER:
        @pl.when(z_dev(d)[0] < OWN_A)
        def _():
            z_copy(pa.at[z_dev(d)[0]], qa.at[d], s2a, r2a, d).start()

    for copy in first_b.values():
        copy.wait_recv()
    part = sb[pl.ds(z * OWN_B, OWN_B)].astype(jnp.float32)
    for d in range(1, NZ):
        part = part + rb[d].astype(jnp.float32)
    pb[...] = part
    for d in Y_ORDER:
        @pl.when(y_dev(d)[0] < OWN_B)
        def _():
            y_copy(pb.at[y_dev(d)[0]], qb.at[d], s2b, r2b, d).start()

    mine_a = y * OWN_A + z
    mine_b = ALL_A + z * OWN_B + y

    @pl.when(y < OWN_B)
    def _():
        for d in range(1, NY):
            y_copy(pb.at[0], qb.at[d], s2b, r2b, d).wait_recv()
        whole = pb[y]
        for d in range(1, NY):
            whole = whole + qb[d]
        fin[mine_b] = (whole * scale).astype(jnp.bfloat16)
        for d in Y_ORDER:
            y_copy(fin.at[mine_b], fin.at[mine_b], s3b, r3b, d).start()

    @pl.when(z < OWN_A)
    def _():
        for d in range(1, NZ):
            z_copy(pa.at[0], qa.at[d], s2a, r2a, d).wait_recv()
        whole = pa[z]
        for d in range(1, NZ):
            whole = whole + qa[d]
        fin[mine_a] = (whole * scale).astype(jnp.bfloat16)
        for d in Z_ORDER:
            z_copy(fin.at[mine_a], fin.at[mine_a], s3a, r3a, d).start()

    def hand_on_b(owner):
        piece = fin.at[ALL_A + z * OWN_B + owner]
        for d in Z_ORDER:
            z_copy(piece, piece, s4b, r4b, d).start()

    def hand_on_a(owner):
        piece = fin.at[y * OWN_A + owner]
        for d in Y_ORDER:
            y_copy(piece, piece, s4a, r4a, d).start()

    @pl.when(y < OWN_B)
    def _():
        hand_on_b(y)

    for d in Y_NEAR:
        owner = lax.rem(y + NY - d, NY)

        @pl.when(owner < OWN_B)
        def _():
            piece = fin.at[ALL_A + z * OWN_B + owner]
            y_copy(piece, piece, s3b, r3b, d).wait_recv()
            hand_on_b(owner)

    @pl.when(z < OWN_A)
    def _():
        hand_on_a(z)

    for d in Z_NEAR:
        owner = lax.rem(z + NZ - d, NZ)

        @pl.when(owner < OWN_A)
        def _():
            piece = fin.at[y * OWN_A + owner]
            z_copy(piece, piece, s3a, r3a, d).wait_recv()
            hand_on_a(owner)

    backward(1)

    for copy in [*first_a.values(), *first_b.values()]:
        copy.wait_send()
    for d in range(1, NZ):
        @pl.when(z_dev(d)[0] < OWN_A)
        def _():
            z_copy(pa.at[0], qa.at[d], s2a, r2a, d).wait_send()
    for d in range(1, NY):
        @pl.when(y_dev(d)[0] < OWN_B)
        def _():
            y_copy(pb.at[0], qb.at[d], s2b, r2b, d).wait_send()

    @pl.when(z < OWN_A)
    def _():
        for d in range(1, NZ):
            z_copy(fin.at[mine_a], fin.at[mine_a], s3a, r3a, d).wait_send()

    @pl.when(y < OWN_B)
    def _():
        for d in range(1, NY):
            y_copy(fin.at[mine_b], fin.at[mine_b], s3b, r3b, d).wait_send()

    block = fin.at[pl.ds(y * OWN_A, OWN_A)]
    for d in Y_NEAR:
        landed = fin.at[pl.ds(lax.rem(y + NY - d, NY) * OWN_A, OWN_A)]
        y_copy(block, block, s4a, r4a, d).wait_send()
        y_copy(landed, landed, s4a, r4a, d).wait_recv()
    block = fin.at[pl.ds(ALL_A + z * OWN_B, OWN_B)]
    for d in Z_NEAR:
        landed = fin.at[pl.ds(ALL_A + lax.rem(z + NZ - d, NZ) * OWN_B, OWN_B)]
        z_copy(block, block, s4b, r4b, d).wait_send()
        z_copy(landed, landed, s4b, r4b, d).wait_recv()
    for c in range(3):
        lanes = slice(128 * c, 128 * c + 128)
        cut = min(max(USED_A - 54 * c, 0), 54)
        if cut > 0:
            sum_out[0:8 * cut, lanes] = fin[54 * c:54 * c + cut].astype(jnp.float32).reshape(8 * cut, 128)
        if cut < 54:
            at = ALL_A + 54 * c + cut - USED_A
            sum_out[8 * cut:432, lanes] = fin[at:at + 54 - cut].astype(jnp.float32).reshape(8 * (54 - cut), 128)


def shards(latent_grad, features, head_weight):
    frames, rows_here, width, channels = features.shape
    cells = frames * rows_here * width
    scale = 1.0 / math.sqrt(cells * NY * NZ)
    bf, f32 = jnp.bfloat16, jnp.float32
    dma = pltpu.SemaphoreType.DMA
    vmem = pl.BlockSpec(memory_space=pltpu.VMEM)
    hbm = pl.BlockSpec(memory_space=pl.ANY)
    grad, total = pl.pallas_call(
        lambda *refs: kernel(scale, *refs),
        out_shape=(
            pltpu.VMEM((cells, channels), bf),
            pltpu.VMEM((432, 384), f32),
        ),
        in_specs=[hbm, hbm, hbm],
        out_specs=(vmem, vmem),
        scratch_shapes=[
            pltpu.VMEM((432, 384), bf),
            pltpu.VMEM((cells, channels), bf),
            pltpu.VMEM((cells, channels), bf),
            pltpu.VMEM((cells, channels), f32),
            pltpu.VMEM((4, 8, 1024), f32),
            pltpu.VMEM((3 * GROUPS, NZ, 8, 128), bf),
            pltpu.VMEM((NY, 8, 1408), bf),
            pltpu.VMEM((NZ, 3 * GROUPS, 8, 128), bf),
            pltpu.VMEM((256, 256), bf),
            pltpu.VMEM((8, 128, 128), f32),
            pltpu.VMEM((2, 384, 128), f32),
            pltpu.VMEM((12, 64, 128), f32),
            pltpu.VMEM((576, 1152), bf),
            pltpu.VMEM((ALL_A, 8, 128), bf),
            pltpu.VMEM((NZ * OWN_B, 8, 128), bf),
            pltpu.VMEM((NY, OWN_A, 8, 128), bf),
            pltpu.VMEM((NZ, OWN_B, 8, 128), bf),
            pltpu.VMEM((OWN_A, 8, 128), f32),
            pltpu.VMEM((NZ, 8, 128), f32),
            pltpu.VMEM((OWN_B, 8, 128), f32),
            pltpu.VMEM((NY, 8, 128), f32),
            pltpu.VMEM((ALL_A + NZ * OWN_B, 8, 128), bf),
            dma((3,)), pltpu.SemaphoreType.REGULAR((NZ,)),
            dma((NY,)), dma((NY,)), dma((GROUPS, NZ)), dma((GROUPS, NZ)),
            dma((NY,)), dma((NY,)), dma((NZ,)), dma((NZ,)),
            dma((NZ,)), dma((NZ,)), dma((NY,)), dma((NY,)),
            dma((NZ,)), dma((NZ,)), dma((NY,)), dma((NY,)),
            dma((NY,)), dma((NY,)), dma((NZ,)), dma((NZ,)),
        ],
        compiler_params=pltpu.CompilerParams(collective_id=0, has_side_effects=True),
        name="encoder_head_backward",
    )(latent_grad.T, features.reshape(cells, channels), head_weight)
    return grad.reshape(features.shape), total


def solution(mesh):
    return jax.shard_map(
        shards,
        mesh=mesh,
        in_specs=(P(("dp", "tm"), "rows"), P(("dp", "tm"), "rows", None, None), P()),
        out_specs=(P(("dp", "tm"), "rows", None, None), P("dp", None)),
        check_vma=False,
    )
```

```python
import math

import jax
import jax.numpy as jnp
from jax import lax
from jax.experimental import pallas as pl
from jax.experimental.pallas import tpu as pltpu
from jax.sharding import PartitionSpec as P

NY = 8
NZ = 16
OWN_A = 15
OWN_B = 3
ALL_A = 120
USED_A = 114
MESH = pl.DeviceIdType.MESH
Y_ORDER = (4, 3, 5, 2, 6, 1, 7)
SLOTS = (0, 1, 7, 2, 6, 3, 5, 4)
Z_LOWER = (7, 6, 8, 5, 9, 4, 10, 3, 11, 2, 12, 1, 13, 0, 14)
GROUPS = 2
Y_NEAR = (1, 7, 2, 6, 3, 5, 4)
Z_NEAR = (1, 15, 2, 14, 3, 13, 4, 12, 5, 11, 6, 10, 7, 9, 8)
Z_ORDER = (8, 7, 9, 6, 10, 5, 11, 4, 12, 3, 13, 2, 14, 1, 15)


def kernel(scale, lat_hbm, feat, weight_hbm, grad_out, sum_out, weight, xf, act, dsl, lp, pk, rx1, rx2, perm, ts, os_, gt, cols, sa, sb, ra, rb, pa, qa, pb, qb, fin, in_sem, ready, sy, ry, sz, rz, s1a, r1a, s1b, r1b, s2a, r2a, s2b, r2b, s3a, r3a, s3b, r3b, s4a, r4a, s4b, r4b):
    tm = lax.axis_index("tm")
    rows = lax.axis_index("rows")
    y = lax.div(tm, 2)
    zh = lax.rem(tm, 2)
    z = zh * 8 + rows

    def y_dev(d):
        other = lax.rem(y + d, NY)
        return other, {"tm": other * 2 + zh}

    def z_dev(d):
        other = lax.rem(z + d, NZ)
        return other, {"tm": y * 2 + lax.div(other, 8), "rows": lax.rem(other, 8)}

    def z_at(other):
        return {"tm": y * 2 + other // 8, "rows": other % 8}

    def window(other):
        first_tile = jnp.minimum(lax.div(9 * other, 2), 28)
        return lat_hbm.at[:, pl.ds(pl.multiple_of(first_tile * 128, 128), 1024)]

    own = pltpu.make_async_copy(window(y), rx1.at[0, :, 0:1024], in_sem.at[0])
    own.start()
    load = pltpu.make_async_copy(feat, xf, in_sem.at[1])
    load.start()
    load_weight = pltpu.make_async_copy(weight_hbm, weight, in_sem.at[2])
    load_weight.start()

    barrier = pltpu.get_barrier_semaphore()
    for d in range(1, NY):
        pl.semaphore_signal(barrier, inc=1, device_id=y_dev(d)[1], device_id_type=MESH)
    for other in range(1, NZ):
        @pl.when(other > z)
        def _():
            pl.semaphore_signal(barrier, inc=1, device_id=z_at(other), device_id_type=MESH)
    rx1[:, :, 1024:1408] = jnp.zeros((NY, 8, 384), jnp.bfloat16)
    lp[:, :, 0:128] = jnp.zeros((4, 8, 128), jnp.float32)
    pl.semaphore_wait(barrier, NY - 1 + z)

    first = [None] * NY
    for slot in range(1, NY):
        other, dev = y_dev(SLOTS[slot])
        copy = pltpu.make_async_remote_copy(window(other), rx1.at[slot, :, 0:1024], sy.at[slot], ry.at[slot], device_id=dev, device_id_type=MESH)
        copy.start()
        first[slot] = copy
    for other in range(NZ - 1):
        @pl.when(other < z)
        def _():
            pl.semaphore_signal(ready.at[z], inc=1, device_id=z_at(other), device_id_type=MESH)

    lane8 = lax.broadcasted_iota(jnp.int32, (8, 128), 1)
    base = pl.multiple_of(jnp.where(y == NY - 1, 384, 0), 128)
    odd = lax.rem(y, 2) == 1

    def pack(group):
        for s in range(4):
            tiles = [rx1[4 * group + s, :, pl.ds(base + 128 * j, 128)].astype(jnp.float32) for j in range(8)]
            turned = [pltpu.roll(tile, 64, 1) for tile in tiles]
            for j in range(7):
                lp[s, :, 128 * j + 128:128 * j + 256] = jnp.where(odd, jnp.where(lane8 < 64, turned[j], turned[j + 1]), tiles[j])
        for zd in range(NZ):
            values = [None] * 3
            for n in range(16):
                s, tt = n // 4, n % 4
                start = 128 + 288 * (zd // 8) + 144 * tt + 18 * (zd % 8) - 3
                move = 24 * n - start
                for v in range(start // 128, (start + 23) // 128 + 1):
                    tile = lp[s, :, 128 * v:128 * v + 128]
                    shift = move % 128
                    tile = pltpu.roll(tile, shift, 1) if shift else tile
                    lo = max(24 * n, 128 * v + move)
                    hi = min(24 * n + 24, 128 * v + 128 + move)
                    for j in range(lo // 128, (hi - 1) // 128 + 1):
                        at = max(lo - 128 * j, 0)
                        values[j] = tile if at == 0 else jnp.where(lane8 < at, values[j], tile)
            for j in range(3):
                pk[3 * group + j, zd] = values[j].astype(jnp.bfloat16)

    def part_copy(group, other, source):
        lo, hi = 3 * group, 3 * group + 3
        return pltpu.make_async_remote_copy(pk.at[lo:hi, other], rx2.at[source, lo:hi], sz.at[group, other], rz.at[group, source], device_id=z_at(other), device_id_type=MESH)

    def whole_copy(other, source):
        return pltpu.make_async_remote_copy(pk.at[:, other], rx2.at[source], sz.at[0, other], rz.at[0, source], device_id=z_at(other), device_id_type=MESH)

    def forward(group):
        for slot in range(4 * group, 4 * group + 4):
            (own.wait if slot == 0 else first[slot].wait_recv)()
        pack(group)
        for other in Z_LOWER:
            @pl.when(other < z)
            def _():
                part_copy(group, other, z).start()

    row = lax.broadcasted_iota(jnp.int32, (256, 256), 0)
    col = lax.broadcasted_iota(jnp.int32, (256, 256), 1)
    slot = (row >> 3) & 7
    back = jnp.where((slot & 1) == 1, (slot + 1) >> 1, 8 - (slot >> 1))
    source = ((y + 8 - back) & 7) * 2 + ((row >> 6) & 1)
    token = jnp.where(row < 128, 15 - source, source + 16)
    target = ((row >> 2) & 1) * 128 + ((row >> 1) & 1) * 64 + token * 2 + (row & 1)
    perm[...] = jnp.where(col == target, 1.0, 0.0).astype(jnp.bfloat16)

    forward(0)
    forward(1)
    load.wait()

    def silu(step, carry):
        at = pl.ds(pl.multiple_of(step * 64, 64), 64)
        x = xf[at, :].astype(jnp.float32)
        sig = 1.0 / (1.0 + jnp.exp(-x))
        act[at, :] = (x * sig).astype(jnp.bfloat16)
        dsl[at, :] = sig * (1.0 + x * (1.0 - sig))
        return carry

    lax.fori_loop(0, 36, silu, 0)
    for other in range(1, NZ):
        @pl.when(other > z)
        def _():
            pl.semaphore_wait(ready.at[other], 1)
            whole_copy(other, z).start()
    rx2[z] = pk[:, z]

    for other in range(NZ):
        @pl.when(other < z)
        def _():
            whole_copy(other, other).wait_recv()
            for group in range(GROUPS):
                part_copy(group, other, other).wait_send()

        @pl.when(other > z)
        def _():
            for group in range(GROUPS):
                part_copy(group, other, other).wait_recv()
            whole_copy(other, other).wait_send()
    for slot in range(1, NY):
        first[slot].wait_send()

    def unpack(zs):
        parts = []
        for group in range(GROUPS):
            t0, t1, t2 = [rx2[zs, 3 * group + j].astype(jnp.float32) for j in range(3)]
            parts.append(t0)
            parts.append(jnp.where(lane8 < 32, pltpu.roll(t0, 32, 1), pltpu.roll(t1, 32, 1)))
            parts.append(jnp.where(lane8 < 64, pltpu.roll(t1, 64, 1), pltpu.roll(t2, 64, 1)))
            parts.append(pltpu.roll(t2, 96, 1))
        return parts

    for r in range(8):
        ts[r] = jnp.concatenate(unpack(r) + unpack(8 + r), axis=0).T
    for r in range(8):
        even = ts[r, pl.ds(0, 48, stride=2), :]
        odds = ts[r, pl.ds(1, 48, stride=2), :]
        left = jnp.concatenate([even, odds], axis=1).astype(jnp.bfloat16)
        moved = jnp.dot(left, perm[...], preferred_element_type=jnp.float32)
        os_[0, r * 48:(r + 1) * 48, :] = moved[:, 0:128]
        os_[1, r * 48:(r + 1) * 48, :] = moved[:, 128:256]
    top = rows == 0
    bottom = rows == 7
    for t in range(4):
        for g in range(4):
            for e in range(2):
                k0, k1, k2 = [os_[e, pl.ds(t * 12 + 3 * g + k, 8, stride=48), :] for k in range(3)]
                at = pl.ds(t * 16 + e, 8, stride=2)
                k1_64 = pltpu.roll(k1, 64, 1)
                k2_96 = pltpu.roll(k2, 96, 1)
                k0_32 = pltpu.roll(k0, 32, 1)
                v0 = jnp.where(lane8 < 64, k0, jnp.where(lane8 < 96, k1_64, k0_32))
                v1 = jnp.where(lane8 < 64, jnp.where(lane8 < 32, k0_32, pltpu.roll(k1, 96, 1)), jnp.where(lane8 < 96, pltpu.roll(k1, 32, 1), k2_96))
                v2 = jnp.where(lane8 < 32, k2_96, jnp.where(lane8 < 64, k1_64, k2))
                if g == 0:
                    v0 = jnp.where(top, 0.0, v0)
                    v1 = jnp.where(jnp.logical_and(top, lane8 < 64), 0.0, v1)
                if g == 3:
                    v1 = jnp.where(jnp.logical_and(bottom, lane8 >= 64), 0.0, v1)
                    v2 = jnp.where(bottom, 0.0, v2)
                gt[3 * g, at, :] = v0
                gt[3 * g + 1, at, :] = v1
                gt[3 * g + 2, at, :] = v2

    place = lax.rem(lax.broadcasted_iota(jnp.int32, (16, 1152), 1), 96)
    for t in range(4):
        grid = jnp.concatenate([gt[v, 16 * t:16 * t + 16, :] for v in range(12)], axis=1)
        for kh in range(3):
            for kw in range(3):
                off = 192 + (1 - kh) * 96 + 1 - kw
                block = pltpu.roll(grid, 1536 - off, 1)[:, 0:1152]
                if kw == 0:
                    block = jnp.where(place == 95, 0.0, block)
                if kw == 2:
                    block = jnp.where(place == 0, 0.0, block)
                at = (3 - t) * 144 + (kh * 3 + kw) * 16
                cols[at:at + 16, :] = block.astype(jnp.bfloat16)

    def y_copy(source, target, ssem, rsem, d):
        return pltpu.make_async_remote_copy(source, target, ssem.at[d], rsem.at[d], device_id=y_dev(d)[1], device_id_type=MESH)

    def z_copy(source, target, ssem, rsem, d):
        return pltpu.make_async_remote_copy(source, target, ssem.at[d], rsem.at[d], device_id=z_dev(d)[1], device_id_type=MESH)

    def weight_part(c):
        lanes = slice(128 * c, 128 * c + 128)
        total = jnp.dot(cols[144:576, :], act[0:1152, lanes], preferred_element_type=jnp.float32)
        total = total + jnp.dot(cols[0:432, :], act[1152:2304, lanes], preferred_element_type=jnp.float32)
        total = total.reshape(54, 8, 128).astype(jnp.bfloat16)
        cut = min(max(USED_A - 54 * c, 0), 54)
        if cut > 0:
            sa[54 * c:54 * c + cut] = total[0:cut]
        if cut < 54:
            at = 54 * c + cut - USED_A
            sb[at:at + 54 - cut] = total[cut:54]

    weight_part(2)
    first_b = {d: z_copy(sb.at[pl.ds(z_dev(d)[0] * OWN_B, OWN_B)], rb.at[d], s1b, r1b, d) for d in Z_ORDER}
    for copy in first_b.values():
        copy.start()
    weight_part(1)
    weight_part(0)
    sa[USED_A:ALL_A] = jnp.zeros((ALL_A - USED_A, 8, 128), jnp.bfloat16)
    first_a = {d: y_copy(sa.at[pl.ds(y_dev(d)[0] * OWN_A, OWN_A)], ra.at[d], s1a, r1a, d) for d in Y_ORDER}
    for copy in first_a.values():
        copy.start()

    load_weight.wait()

    def backward(t):
        def one(step, carry):
            lanes = pl.ds(pl.multiple_of(step * 384, 128), 384)
            at = pl.ds(pl.multiple_of(t * 1152 + step * 384, 128), 384)
            pre = lax.dot_general(cols[(1 - t) * 144:(1 - t) * 144 + 432, lanes], weight[...], (((0,), (0,)), ((), ())), preferred_element_type=jnp.float32)
            grad_out[at, :] = (pre * dsl[at, :]).astype(jnp.bfloat16)
            return carry

        lax.fori_loop(0, 3, one, 0)

    backward(0)

    for copy in first_a.values():
        copy.wait_recv()
    part = sa[pl.ds(y * OWN_A, OWN_A)].astype(jnp.float32)
    for d in range(1, NY):
        part = part + ra[d].astype(jnp.float32)
    pa[...] = part
    for d in Z_ORDER:
        @pl.when(z_dev(d)[0] < OWN_A)
        def _():
            z_copy(pa.at[z_dev(d)[0]], qa.at[d], s2a, r2a, d).start()

    for copy in first_b.values():
        copy.wait_recv()
    part = sb[pl.ds(z * OWN_B, OWN_B)].astype(jnp.float32)
    for d in range(1, NZ):
        part = part + rb[d].astype(jnp.float32)
    pb[...] = part
    for d in Y_ORDER:
        @pl.when(y_dev(d)[0] < OWN_B)
        def _():
            y_copy(pb.at[y_dev(d)[0]], qb.at[d], s2b, r2b, d).start()

    backward(1)
    mine_a = y * OWN_A + z
    mine_b = ALL_A + z * OWN_B + y

    @pl.when(y < OWN_B)
    def _():
        for d in range(1, NY):
            y_copy(pb.at[0], qb.at[d], s2b, r2b, d).wait_recv()
        whole = pb[y]
        for d in range(1, NY):
            whole = whole + qb[d]
        fin[mine_b] = (whole * scale).astype(jnp.bfloat16)
        for d in Y_ORDER:
            y_copy(fin.at[mine_b], fin.at[mine_b], s3b, r3b, d).start()

    @pl.when(z < OWN_A)
    def _():
        for d in range(1, NZ):
            z_copy(pa.at[0], qa.at[d], s2a, r2a, d).wait_recv()
        whole = pa[z]
        for d in range(1, NZ):
            whole = whole + qa[d]
        fin[mine_a] = (whole * scale).astype(jnp.bfloat16)
        for d in Z_ORDER:
            z_copy(fin.at[mine_a], fin.at[mine_a], s3a, r3a, d).start()

    def hand_on_b(owner):
        piece = fin.at[ALL_A + z * OWN_B + owner]
        for d in Z_ORDER:
            z_copy(piece, piece, s4b, r4b, d).start()

    def hand_on_a(owner):
        piece = fin.at[y * OWN_A + owner]
        for d in Y_ORDER:
            y_copy(piece, piece, s4a, r4a, d).start()

    @pl.when(y < OWN_B)
    def _():
        hand_on_b(y)

    for d in Y_NEAR:
        owner = lax.rem(y + NY - d, NY)

        @pl.when(owner < OWN_B)
        def _():
            piece = fin.at[ALL_A + z * OWN_B + owner]
            y_copy(piece, piece, s3b, r3b, d).wait_recv()
            hand_on_b(owner)

    @pl.when(z < OWN_A)
    def _():
        hand_on_a(z)

    for d in Z_NEAR:
        owner = lax.rem(z + NZ - d, NZ)

        @pl.when(owner < OWN_A)
        def _():
            piece = fin.at[y * OWN_A + owner]
            z_copy(piece, piece, s3a, r3a, d).wait_recv()
            hand_on_a(owner)


    for copy in [*first_a.values(), *first_b.values()]:
        copy.wait_send()
    for d in range(1, NZ):
        @pl.when(z_dev(d)[0] < OWN_A)
        def _():
            z_copy(pa.at[0], qa.at[d], s2a, r2a, d).wait_send()
    for d in range(1, NY):
        @pl.when(y_dev(d)[0] < OWN_B)
        def _():
            y_copy(pb.at[0], qb.at[d], s2b, r2b, d).wait_send()

    @pl.when(z < OWN_A)
    def _():
        for d in range(1, NZ):
            z_copy(fin.at[mine_a], fin.at[mine_a], s3a, r3a, d).wait_send()

    @pl.when(y < OWN_B)
    def _():
        for d in range(1, NY):
            y_copy(fin.at[mine_b], fin.at[mine_b], s3b, r3b, d).wait_send()

    block = fin.at[pl.ds(y * OWN_A, OWN_A)]
    for d in Y_NEAR:
        landed = fin.at[pl.ds(lax.rem(y + NY - d, NY) * OWN_A, OWN_A)]
        y_copy(block, block, s4a, r4a, d).wait_send()
        y_copy(landed, landed, s4a, r4a, d).wait_recv()
    block = fin.at[pl.ds(ALL_A + z * OWN_B, OWN_B)]
    for d in Z_NEAR:
        landed = fin.at[pl.ds(ALL_A + lax.rem(z + NZ - d, NZ) * OWN_B, OWN_B)]
        z_copy(block, block, s4b, r4b, d).wait_send()
        z_copy(landed, landed, s4b, r4b, d).wait_recv()
    for c in range(3):
        lanes = slice(128 * c, 128 * c + 128)
        cut = min(max(USED_A - 54 * c, 0), 54)
        if cut > 0:
            sum_out[0:8 * cut, lanes] = fin[54 * c:54 * c + cut].astype(jnp.float32).reshape(8 * cut, 128)
        if cut < 54:
            at = ALL_A + 54 * c + cut - USED_A
            sum_out[8 * cut:432, lanes] = fin[at:at + 54 - cut].astype(jnp.float32).reshape(8 * (54 - cut), 128)


def store(grad, total, grad_out, total_out, sem):
    copies = [pltpu.make_async_copy(total, total_out, sem.at[0])]
    for i in range(4):
        at = pl.ds(576 * i, 576)
        copies.append(pltpu.make_async_copy(grad.at[at], grad_out.at[at], sem.at[1 + i]))
    for copy in copies:
        copy.start()
    for copy in copies:
        copy.wait()


def shards(latent_grad, features, head_weight):
    frames, rows_here, width, channels = features.shape
    cells = frames * rows_here * width
    scale = 1.0 / math.sqrt(cells * NY * NZ)
    bf, f32 = jnp.bfloat16, jnp.float32
    dma = pltpu.SemaphoreType.DMA
    vmem = pl.BlockSpec(memory_space=pltpu.VMEM)
    hbm = pl.BlockSpec(memory_space=pl.ANY)
    grad, total = pl.pallas_call(
        lambda *refs: kernel(scale, *refs),
        out_shape=(
            pltpu.VMEM((cells, channels), bf),
            pltpu.VMEM((432, 384), f32),
        ),
        in_specs=[hbm, hbm, hbm],
        out_specs=(vmem, vmem),
        scratch_shapes=[
            pltpu.VMEM((432, 384), bf),
            pltpu.VMEM((cells, channels), bf),
            pltpu.VMEM((cells, channels), bf),
            pltpu.VMEM((cells, channels), f32),
            pltpu.VMEM((4, 8, 1024), f32),
            pltpu.VMEM((3 * GROUPS, NZ, 8, 128), bf),
            pltpu.VMEM((NY, 8, 1408), bf),
            pltpu.VMEM((NZ, 3 * GROUPS, 8, 128), bf),
            pltpu.VMEM((256, 256), bf),
            pltpu.VMEM((8, 128, 128), f32),
            pltpu.VMEM((2, 384, 128), f32),
            pltpu.VMEM((12, 64, 128), f32),
            pltpu.VMEM((576, 1152), bf),
            pltpu.VMEM((ALL_A, 8, 128), bf),
            pltpu.VMEM((NZ * OWN_B, 8, 128), bf),
            pltpu.VMEM((NY, OWN_A, 8, 128), bf),
            pltpu.VMEM((NZ, OWN_B, 8, 128), bf),
            pltpu.VMEM((OWN_A, 8, 128), f32),
            pltpu.VMEM((NZ, 8, 128), f32),
            pltpu.VMEM((OWN_B, 8, 128), f32),
            pltpu.VMEM((NY, 8, 128), f32),
            pltpu.VMEM((ALL_A + NZ * OWN_B, 8, 128), bf),
            dma((3,)), pltpu.SemaphoreType.REGULAR((NZ,)),
            dma((NY,)), dma((NY,)), dma((GROUPS, NZ)), dma((GROUPS, NZ)),
            dma((NY,)), dma((NY,)), dma((NZ,)), dma((NZ,)),
            dma((NZ,)), dma((NZ,)), dma((NY,)), dma((NY,)),
            dma((NZ,)), dma((NZ,)), dma((NY,)), dma((NY,)),
            dma((NY,)), dma((NY,)), dma((NZ,)), dma((NZ,)),
        ],
        compiler_params=pltpu.CompilerParams(collective_id=0, has_side_effects=True),
        name="encoder_head_backward",
    )(latent_grad.T, features.reshape(cells, channels), head_weight)
    grad, total = pl.pallas_call(
        store,
        out_shape=(
            jax.ShapeDtypeStruct((cells, channels), bf),
            jax.ShapeDtypeStruct((432, 384), f32),
        ),
        in_specs=[hbm, hbm],
        out_specs=(hbm, hbm),
        scratch_shapes=[dma((5,))],
        name="store_results",
    )(*[pltpu.with_memory_space_constraint(x, pltpu.VMEM) for x in (grad, total)])
    return grad.reshape(features.shape), total


def solution(mesh):
    return jax.shard_map(
        shards,
        mesh=mesh,
        in_specs=(P(("dp", "tm"), "rows"), P(("dp", "tm"), "rows", None, None), P()),
        out_specs=(P(("dp", "tm"), "rows", None, None), P("dp", None)),
        check_vma=False,
    )
```

```python
import math

import jax
import jax.numpy as jnp
from jax import lax
from jax.experimental import pallas as pl
from jax.experimental.pallas import tpu as pltpu
from jax.sharding import PartitionSpec as P

NY = 8
NZ = 16
OWN_A = 15
OWN_B = 3
ALL_A = 120
USED_A = 114
MESH = pl.DeviceIdType.MESH
Y_ORDER = (4, 3, 5, 2, 6, 1, 7)
SLOTS = (0, 1, 7, 2, 6, 3, 5, 4)
Z_LOWER = (7, 6, 8, 5, 9, 4, 10, 3, 11, 2, 12, 1, 13, 0, 14)
GROUPS = 2
Y_NEAR = (1, 7, 2, 6, 3, 5, 4)
Z_NEAR = (1, 15, 2, 14, 3, 13, 4, 12, 5, 11, 6, 10, 7, 9, 8)
Z_ORDER = (8, 7, 9, 6, 10, 5, 11, 4, 12, 3, 13, 2, 14, 1, 15)


def kernel(scale, lat_hbm, feat, weight_hbm, grad_out, sum_out, weight, xf, act, dsl, lp, pk, rx1, rx2, perm, ts, os_, gt, cols, sa, sb, ra, rb, pa, qa, pb, qb, fin, in_sem, ready, sy, ry, sz, rz, s1a, r1a, s1b, r1b, s2a, r2a, s2b, r2b, s3a, r3a, s3b, r3b, s4a, r4a, s4b, r4b):
    tm = lax.axis_index("tm")
    rows = lax.axis_index("rows")
    y = lax.div(tm, 2)
    zh = lax.rem(tm, 2)
    z = zh * 8 + rows

    def y_dev(d):
        other = lax.rem(y + d, NY)
        return other, {"tm": other * 2 + zh}

    def z_dev(d):
        other = lax.rem(z + d, NZ)
        return other, {"tm": y * 2 + lax.div(other, 8), "rows": lax.rem(other, 8)}

    def z_at(other):
        return {"tm": y * 2 + other // 8, "rows": other % 8}

    def window(other):
        first_tile = jnp.minimum(lax.div(9 * other, 2), 28)
        return lat_hbm.at[:, pl.ds(pl.multiple_of(first_tile * 128, 128), 1024)]

    own = pltpu.make_async_copy(window(y), rx1.at[0, :, 0:1024], in_sem.at[0])
    own.start()
    load = pltpu.make_async_copy(feat, xf, in_sem.at[1])
    load.start()
    load_weight = pltpu.make_async_copy(weight_hbm, weight, in_sem.at[2])
    load_weight.start()

    barrier = pltpu.get_barrier_semaphore()
    for d in range(1, NY):
        pl.semaphore_signal(barrier, inc=1, device_id=y_dev(d)[1], device_id_type=MESH)
    for other in range(1, NZ):
        @pl.when(other > z)
        def _():
            pl.semaphore_signal(barrier, inc=1, device_id=z_at(other), device_id_type=MESH)
    rx1[:, :, 1024:1408] = jnp.zeros((NY, 8, 384), jnp.bfloat16)
    lp[:, :, 0:128] = jnp.zeros((4, 8, 128), jnp.float32)
    pl.semaphore_wait(barrier, NY - 1 + z)

    first = [None] * NY
    for slot in reversed(range(1, NY)):
        other, dev = y_dev(SLOTS[slot])
        copy = pltpu.make_async_remote_copy(window(other), rx1.at[slot, :, 0:1024], sy.at[slot], ry.at[slot], device_id=dev, device_id_type=MESH)
        copy.start()
        first[slot] = copy
    for other in range(NZ - 1):
        @pl.when(other < z)
        def _():
            pl.semaphore_signal(ready.at[z], inc=1, device_id=z_at(other), device_id_type=MESH)

    lane8 = lax.broadcasted_iota(jnp.int32, (8, 128), 1)
    base = pl.multiple_of(jnp.where(y == NY - 1, 384, 0), 128)
    odd = lax.rem(y, 2) == 1

    def pack(group):
        for s in range(4):
            tiles = [rx1[4 * group + s, :, pl.ds(base + 128 * j, 128)].astype(jnp.float32) for j in range(8)]
            turned = [pltpu.roll(tile, 64, 1) for tile in tiles]
            for j in range(7):
                lp[s, :, 128 * j + 128:128 * j + 256] = jnp.where(odd, jnp.where(lane8 < 64, turned[j], turned[j + 1]), tiles[j])
        for zd in range(NZ):
            values = [None] * 3
            for n in range(16):
                s, tt = n // 4, n % 4
                start = 128 + 288 * (zd // 8) + 144 * tt + 18 * (zd % 8) - 3
                move = 24 * n - start
                for v in range(start // 128, (start + 23) // 128 + 1):
                    tile = lp[s, :, 128 * v:128 * v + 128]
                    shift = move % 128
                    tile = pltpu.roll(tile, shift, 1) if shift else tile
                    lo = max(24 * n, 128 * v + move)
                    hi = min(24 * n + 24, 128 * v + 128 + move)
                    for j in range(lo // 128, (hi - 1) // 128 + 1):
                        at = max(lo - 128 * j, 0)
                        values[j] = tile if at == 0 else jnp.where(lane8 < at, values[j], tile)
            for j in range(3):
                pk[3 * group + j, zd] = values[j].astype(jnp.bfloat16)

    def part_copy(group, other, source):
        lo, hi = 3 * group, 3 * group + 3
        return pltpu.make_async_remote_copy(pk.at[lo:hi, other], rx2.at[source, lo:hi], sz.at[group, other], rz.at[group, source], device_id=z_at(other), device_id_type=MESH)

    def whole_copy(other, source):
        return pltpu.make_async_remote_copy(pk.at[:, other], rx2.at[source], sz.at[0, other], rz.at[0, source], device_id=z_at(other), device_id_type=MESH)

    def forward(group):
        for slot in range(4 * group, 4 * group + 4):
            (own.wait if slot == 0 else first[slot].wait_recv)()
        pack(group)
        for other in Z_LOWER:
            @pl.when(other < z)
            def _():
                part_copy(group, other, z).start()

    row = lax.broadcasted_iota(jnp.int32, (256, 256), 0)
    col = lax.broadcasted_iota(jnp.int32, (256, 256), 1)
    slot = (row >> 3) & 7
    back = jnp.where((slot & 1) == 1, (slot + 1) >> 1, 8 - (slot >> 1))
    source = ((y + 8 - back) & 7) * 2 + ((row >> 6) & 1)
    token = jnp.where(row < 128, 15 - source, source + 16)
    target = ((row >> 2) & 1) * 128 + ((row >> 1) & 1) * 64 + token * 2 + (row & 1)
    perm[...] = jnp.where(col == target, 1.0, 0.0).astype(jnp.bfloat16)

    forward(0)
    forward(1)
    load.wait()

    def silu(step, carry):
        at = pl.ds(pl.multiple_of(step * 64, 64), 64)
        x = xf[at, :].astype(jnp.float32)
        sig = 1.0 / (1.0 + jnp.exp(-x))
        act[at, :] = (x * sig).astype(jnp.bfloat16)
        dsl[at, :] = sig * (1.0 + x * (1.0 - sig))
        return carry

    lax.fori_loop(0, 36, silu, 0)
    for other in range(1, NZ):
        @pl.when(other > z)
        def _():
            pl.semaphore_wait(ready.at[other], 1)
            whole_copy(other, z).start()
    rx2[z] = pk[:, z]

    for other in range(NZ):
        @pl.when(other < z)
        def _():
            whole_copy(other, other).wait_recv()
            for group in range(GROUPS):
                part_copy(group, other, other).wait_send()

        @pl.when(other > z)
        def _():
            for group in range(GROUPS):
                part_copy(group, other, other).wait_recv()
            whole_copy(other, other).wait_send()
    for slot in range(1, NY):
        first[slot].wait_send()

    def unpack(zs):
        parts = []
        for group in range(GROUPS):
            t0, t1, t2 = [rx2[zs, 3 * group + j].astype(jnp.float32) for j in range(3)]
            parts.append(t0)
            parts.append(jnp.where(lane8 < 32, pltpu.roll(t0, 32, 1), pltpu.roll(t1, 32, 1)))
            parts.append(jnp.where(lane8 < 64, pltpu.roll(t1, 64, 1), pltpu.roll(t2, 64, 1)))
            parts.append(pltpu.roll(t2, 96, 1))
        return parts

    for r in range(8):
        ts[r] = jnp.concatenate(unpack(r) + unpack(8 + r), axis=0).T
    for r in range(8):
        even = ts[r, pl.ds(0, 48, stride=2), :]
        odds = ts[r, pl.ds(1, 48, stride=2), :]
        left = jnp.concatenate([even, odds], axis=1).astype(jnp.bfloat16)
        moved = jnp.dot(left, perm[...], preferred_element_type=jnp.float32)
        os_[0, r * 48:(r + 1) * 48, :] = moved[:, 0:128]
        os_[1, r * 48:(r + 1) * 48, :] = moved[:, 128:256]
    top = rows == 0
    bottom = rows == 7
    for t in range(4):
        for g in range(4):
            for e in range(2):
                k0, k1, k2 = [os_[e, pl.ds(t * 12 + 3 * g + k, 8, stride=48), :] for k in range(3)]
                at = pl.ds(t * 16 + e, 8, stride=2)
                k1_64 = pltpu.roll(k1, 64, 1)
                k2_96 = pltpu.roll(k2, 96, 1)
                k0_32 = pltpu.roll(k0, 32, 1)
                v0 = jnp.where(lane8 < 64, k0, jnp.where(lane8 < 96, k1_64, k0_32))
                v1 = jnp.where(lane8 < 64, jnp.where(lane8 < 32, k0_32, pltpu.roll(k1, 96, 1)), jnp.where(lane8 < 96, pltpu.roll(k1, 32, 1), k2_96))
                v2 = jnp.where(lane8 < 32, k2_96, jnp.where(lane8 < 64, k1_64, k2))
                if g == 0:
                    v0 = jnp.where(top, 0.0, v0)
                    v1 = jnp.where(jnp.logical_and(top, lane8 < 64), 0.0, v1)
                if g == 3:
                    v1 = jnp.where(jnp.logical_and(bottom, lane8 >= 64), 0.0, v1)
                    v2 = jnp.where(bottom, 0.0, v2)
                gt[3 * g, at, :] = v0
                gt[3 * g + 1, at, :] = v1
                gt[3 * g + 2, at, :] = v2

    place = lax.rem(lax.broadcasted_iota(jnp.int32, (16, 1152), 1), 96)
    for t in range(4):
        grid = jnp.concatenate([gt[v, 16 * t:16 * t + 16, :] for v in range(12)], axis=1)
        for kh in range(3):
            for kw in range(3):
                off = 192 + (1 - kh) * 96 + 1 - kw
                block = pltpu.roll(grid, 1536 - off, 1)[:, 0:1152]
                if kw == 0:
                    block = jnp.where(place == 95, 0.0, block)
                if kw == 2:
                    block = jnp.where(place == 0, 0.0, block)
                at = (3 - t) * 144 + (kh * 3 + kw) * 16
                cols[at:at + 16, :] = block.astype(jnp.bfloat16)

    def y_copy(source, target, ssem, rsem, d):
        return pltpu.make_async_remote_copy(source, target, ssem.at[d], rsem.at[d], device_id=y_dev(d)[1], device_id_type=MESH)

    def z_copy(source, target, ssem, rsem, d):
        return pltpu.make_async_remote_copy(source, target, ssem.at[d], rsem.at[d], device_id=z_dev(d)[1], device_id_type=MESH)

    def weight_part(c):
        lanes = slice(128 * c, 128 * c + 128)
        total = jnp.dot(cols[144:576, :], act[0:1152, lanes], preferred_element_type=jnp.float32)
        total = total + jnp.dot(cols[0:432, :], act[1152:2304, lanes], preferred_element_type=jnp.float32)
        total = total.reshape(54, 8, 128).astype(jnp.bfloat16)
        cut = min(max(USED_A - 54 * c, 0), 54)
        if cut > 0:
            sa[54 * c:54 * c + cut] = total[0:cut]
        if cut < 54:
            at = 54 * c + cut - USED_A
            sb[at:at + 54 - cut] = total[cut:54]

    weight_part(2)
    first_b = {d: z_copy(sb.at[pl.ds(z_dev(d)[0] * OWN_B, OWN_B)], rb.at[d], s1b, r1b, d) for d in Z_ORDER}
    for copy in first_b.values():
        copy.start()
    weight_part(1)
    weight_part(0)
    sa[USED_A:ALL_A] = jnp.zeros((ALL_A - USED_A, 8, 128), jnp.bfloat16)
    first_a = {d: y_copy(sa.at[pl.ds(y_dev(d)[0] * OWN_A, OWN_A)], ra.at[d], s1a, r1a, d) for d in Y_ORDER}
    for copy in first_a.values():
        copy.start()

    load_weight.wait()

    def backward(t):
        def one(step, carry):
            lanes = pl.ds(pl.multiple_of(step * 384, 128), 384)
            at = pl.ds(pl.multiple_of(t * 1152 + step * 384, 128), 384)
            pre = lax.dot_general(cols[(1 - t) * 144:(1 - t) * 144 + 432, lanes], weight[...], (((0,), (0,)), ((), ())), preferred_element_type=jnp.float32)
            grad_out[at, :] = (pre * dsl[at, :]).astype(jnp.bfloat16)
            return carry

        lax.fori_loop(0, 3, one, 0)

    backward(0)

    for copy in first_a.values():
        copy.wait_recv()
    part = sa[pl.ds(y * OWN_A, OWN_A)].astype(jnp.float32)
    for d in range(1, NY):
        part = part + ra[d].astype(jnp.float32)
    pa[...] = part
    for d in Z_ORDER:
        @pl.when(z_dev(d)[0] < OWN_A)
        def _():
            z_copy(pa.at[z_dev(d)[0]], qa.at[d], s2a, r2a, d).start()

    for copy in first_b.values():
        copy.wait_recv()
    part = sb[pl.ds(z * OWN_B, OWN_B)].astype(jnp.float32)
    for d in range(1, NZ):
        part = part + rb[d].astype(jnp.float32)
    pb[...] = part
    for d in Y_ORDER:
        @pl.when(y_dev(d)[0] < OWN_B)
        def _():
            y_copy(pb.at[y_dev(d)[0]], qb.at[d], s2b, r2b, d).start()

    backward(1)
    mine_a = y * OWN_A + z
    mine_b = ALL_A + z * OWN_B + y

    @pl.when(y < OWN_B)
    def _():
        for d in range(1, NY):
            y_copy(pb.at[0], qb.at[d], s2b, r2b, d).wait_recv()
        whole = pb[y]
        for d in range(1, NY):
            whole = whole + qb[d]
        fin[mine_b] = (whole * scale).astype(jnp.bfloat16)
        for d in Y_ORDER:
            y_copy(fin.at[mine_b], fin.at[mine_b], s3b, r3b, d).start()

    @pl.when(z < OWN_A)
    def _():
        for d in range(1, NZ):
            z_copy(pa.at[0], qa.at[d], s2a, r2a, d).wait_recv()
        whole = pa[z]
        for d in range(1, NZ):
            whole = whole + qa[d]
        fin[mine_a] = (whole * scale).astype(jnp.bfloat16)
        for d in Z_ORDER:
            z_copy(fin.at[mine_a], fin.at[mine_a], s3a, r3a, d).start()

    def hand_on_b(owner):
        piece = fin.at[ALL_A + z * OWN_B + owner]
        for d in Z_ORDER:
            z_copy(piece, piece, s4b, r4b, d).start()

    def hand_on_a(owner):
        piece = fin.at[y * OWN_A + owner]
        for d in Y_ORDER:
            y_copy(piece, piece, s4a, r4a, d).start()

    @pl.when(y < OWN_B)
    def _():
        hand_on_b(y)

    for d in Y_NEAR:
        owner = lax.rem(y + NY - d, NY)

        @pl.when(owner < OWN_B)
        def _():
            piece = fin.at[ALL_A + z * OWN_B + owner]
            y_copy(piece, piece, s3b, r3b, d).wait_recv()
            hand_on_b(owner)

    @pl.when(z < OWN_A)
    def _():
        hand_on_a(z)

    for d in Z_NEAR:
        owner = lax.rem(z + NZ - d, NZ)

        @pl.when(owner < OWN_A)
        def _():
            piece = fin.at[y * OWN_A + owner]
            z_copy(piece, piece, s3a, r3a, d).wait_recv()
            hand_on_a(owner)


    for copy in [*first_a.values(), *first_b.values()]:
        copy.wait_send()
    for d in range(1, NZ):
        @pl.when(z_dev(d)[0] < OWN_A)
        def _():
            z_copy(pa.at[0], qa.at[d], s2a, r2a, d).wait_send()
    for d in range(1, NY):
        @pl.when(y_dev(d)[0] < OWN_B)
        def _():
            y_copy(pb.at[0], qb.at[d], s2b, r2b, d).wait_send()

    @pl.when(z < OWN_A)
    def _():
        for d in range(1, NZ):
            z_copy(fin.at[mine_a], fin.at[mine_a], s3a, r3a, d).wait_send()

    @pl.when(y < OWN_B)
    def _():
        for d in range(1, NY):
            y_copy(fin.at[mine_b], fin.at[mine_b], s3b, r3b, d).wait_send()

    block = fin.at[pl.ds(y * OWN_A, OWN_A)]
    for d in Y_NEAR:
        landed = fin.at[pl.ds(lax.rem(y + NY - d, NY) * OWN_A, OWN_A)]
        y_copy(block, block, s4a, r4a, d).wait_send()
        y_copy(landed, landed, s4a, r4a, d).wait_recv()
    block = fin.at[pl.ds(ALL_A + z * OWN_B, OWN_B)]
    for d in Z_NEAR:
        landed = fin.at[pl.ds(ALL_A + lax.rem(z + NZ - d, NZ) * OWN_B, OWN_B)]
        z_copy(block, block, s4b, r4b, d).wait_send()
        z_copy(landed, landed, s4b, r4b, d).wait_recv()
    for c in range(3):
        lanes = slice(128 * c, 128 * c + 128)
        cut = min(max(USED_A - 54 * c, 0), 54)
        if cut > 0:
            sum_out[0:8 * cut, lanes] = fin[54 * c:54 * c + cut].astype(jnp.float32).reshape(8 * cut, 128)
        if cut < 54:
            at = ALL_A + 54 * c + cut - USED_A
            sum_out[8 * cut:432, lanes] = fin[at:at + 54 - cut].astype(jnp.float32).reshape(8 * (54 - cut), 128)


def store(grad, total, grad_out, total_out, sem):
    copies = [pltpu.make_async_copy(total, total_out, sem.at[0])]
    for i in range(4):
        at = pl.ds(576 * i, 576)
        copies.append(pltpu.make_async_copy(grad.at[at], grad_out.at[at], sem.at[1 + i]))
    for copy in copies:
        copy.start()
    for copy in copies:
        copy.wait()


def shards(latent_grad, features, head_weight):
    frames, rows_here, width, channels = features.shape
    cells = frames * rows_here * width
    scale = 1.0 / math.sqrt(cells * NY * NZ)
    bf, f32 = jnp.bfloat16, jnp.float32
    dma = pltpu.SemaphoreType.DMA
    vmem = pl.BlockSpec(memory_space=pltpu.VMEM)
    hbm = pl.BlockSpec(memory_space=pl.ANY)
    grad, total = pl.pallas_call(
        lambda *refs: kernel(scale, *refs),
        out_shape=(
            pltpu.VMEM((cells, channels), bf),
            pltpu.VMEM((432, 384), f32),
        ),
        in_specs=[hbm, hbm, hbm],
        out_specs=(vmem, vmem),
        scratch_shapes=[
            pltpu.VMEM((432, 384), bf),
            pltpu.VMEM((cells, channels), bf),
            pltpu.VMEM((cells, channels), bf),
            pltpu.VMEM((cells, channels), f32),
            pltpu.VMEM((4, 8, 1024), f32),
            pltpu.VMEM((3 * GROUPS, NZ, 8, 128), bf),
            pltpu.VMEM((NY, 8, 1408), bf),
            pltpu.VMEM((NZ, 3 * GROUPS, 8, 128), bf),
            pltpu.VMEM((256, 256), bf),
            pltpu.VMEM((8, 128, 128), f32),
            pltpu.VMEM((2, 384, 128), f32),
            pltpu.VMEM((12, 64, 128), f32),
            pltpu.VMEM((576, 1152), bf),
            pltpu.VMEM((ALL_A, 8, 128), bf),
            pltpu.VMEM((NZ * OWN_B, 8, 128), bf),
            pltpu.VMEM((NY, OWN_A, 8, 128), bf),
            pltpu.VMEM((NZ, OWN_B, 8, 128), bf),
            pltpu.VMEM((OWN_A, 8, 128), f32),
            pltpu.VMEM((NZ, 8, 128), f32),
            pltpu.VMEM((OWN_B, 8, 128), f32),
            pltpu.VMEM((NY, 8, 128), f32),
            pltpu.VMEM((ALL_A + NZ * OWN_B, 8, 128), bf),
            dma((3,)), pltpu.SemaphoreType.REGULAR((NZ,)),
            dma((NY,)), dma((NY,)), dma((GROUPS, NZ)), dma((GROUPS, NZ)),
            dma((NY,)), dma((NY,)), dma((NZ,)), dma((NZ,)),
            dma((NZ,)), dma((NZ,)), dma((NY,)), dma((NY,)),
            dma((NZ,)), dma((NZ,)), dma((NY,)), dma((NY,)),
            dma((NY,)), dma((NY,)), dma((NZ,)), dma((NZ,)),
        ],
        compiler_params=pltpu.CompilerParams(collective_id=0, has_side_effects=True),
        name="encoder_head_backward",
    )(latent_grad.T, features.reshape(cells, channels), head_weight)
    grad, total = pl.pallas_call(
        store,
        out_shape=(
            jax.ShapeDtypeStruct((cells, channels), bf),
            jax.ShapeDtypeStruct((432, 384), f32),
        ),
        in_specs=[hbm, hbm],
        out_specs=(hbm, hbm),
        scratch_shapes=[dma((5,))],
        name="store_results",
    )(*[pltpu.with_memory_space_constraint(x, pltpu.VMEM) for x in (grad, total)])
    return grad.reshape(features.shape), total


def solution(mesh):
    return jax.shard_map(
        shards,
        mesh=mesh,
        in_specs=(P(("dp", "tm"), "rows"), P(("dp", "tm"), "rows", None, None), P()),
        out_specs=(P(("dp", "tm"), "rows", None, None), P("dp", None)),
        check_vma=False,
    )
```
